256 devices in a mesh: section: 8 (over y, core), tensor: 32 (over z, x).
Axes of the slice: x: 4, y: 4, z: 8, core: 2. Of those that a mesh axis runs over, the one named last changes fastest.
Arguments:
- saved_inputs: bfloat16 [8, 4, 256, 1024], P('section', None, 'tensor'), may hold values from -6 to 6
- slot_index: int32 [8, 3], P('section'), may hold values from 0 to 3
- example_lengths: int32 [8, 3, 2], P('section'), may hold values from 1 to 192, 256 in all within a row
- first_grads: bfloat16 [8, 256, 1024], P('section', 'tensor'), may hold values from -6 to 6
- loss_grads: bfloat16 [2, 256, 1024], P(None, 'tensor'), may hold values from -6 to 6
- w_in: bfloat16 [8, 1024, 32768], P('section', None, 'tensor'), may hold values from -0.1875 to 0.1875
- w_out: bfloat16 [8, 32768, 1024], P('section', 'tensor'), may hold values from -0.03125 to 0.03125
Outputs:
- grad_in: bfloat16 [8, 1024, 32768], P('section', None, 'tensor')
- grad_out: bfloat16 [8, 32768, 1024], P('section', 'tensor')
- input_grads: bfloat16 [8, 3, 256, 1024], P('section', None, 'tensor')
The draws below stay inside these ranges and needn't reach their ends.
Inputs may be any that keep to these rules, and one draw needn't show every extreme that they name: `example_lengths`: the 2 lengths of one microbatch sum to 256.
All inputs are finite; a program needn't handle non-finite values.
Results may differ from the reference program's by a relative error of at most 0.0095.
Values may be sent and summed in bfloat16 or wider, within the bound.
No kernel may reach another device: no remote copies, remote signals or barrier semaphores. Data moves between devices by JAX's collectives and lax.ppermute only.
A program may use at most 128 MiB of HBM per device.

```python
import math
import jax
import jax.numpy as jnp
import numpy as np
from jax import lax

D = 1024
FF = 32768
TOK_MB = 256
EXAMPLES = 2
SLOTS = 3
BUF = 4
MOST = 192
SECTIONS = 8


def plant(drawn, stream_key, low, high):
    shape = drawn.shape
    place = [jax.random.randint(jax.random.fold_in(stream_key, axis), (), 0, shape[axis]) for axis in range(len(shape))]
    drawn = drawn.at[tuple(place)].set(low)
    longest = shape.index(max(shape))
    place[longest] = (place[longest] + 1) % shape[longest]
    return drawn.at[tuple(place)].set(high)


def steps_of(own_key, dims, shards, smallest, high):
    def one(axis_at, shards_of):
        draws = jax.random.uniform(jax.random.fold_in(jax.random.fold_in(own_key, 6), axis_at), (shards_of,), jnp.float32, smallest / len(shards), high / len(shards))
        return jnp.repeat(jnp.exp(draws), dims[axis_at] // shards_of).reshape((-1,) + (1,) * (len(dims) - axis_at - 1))

    loudness = one(*shards[0])
    for cut in shards[1:]:
        loudness = loudness * one(*cut)
    return loudness


def split_up(count, total, most, lean):
    loads = [(1 << 20) // math.isqrt(grade ** lean) + 1 for grade in range(2, count + 1)]
    surplus, holding = total - most - (count - 1), [1] * (count - 1)
    while surplus > 0:
        free = [i for i in range(count - 1) if holding[i] < most]
        pool, left = sum([loads[i] for i in free]), surplus
        for i in free:
            addition = min(most - holding[i], max(1, left * loads[i] // pool), surplus)
            holding[i] = holding[i] + addition
            surplus = surplus - addition
    return np.array([most] + holding)


def uneven(rng, count, total, most, skew):
    if count == 2:
        one = jax.random.randint(rng, (), max(1, total - most), min(most, total - 1) + 1)
        return jnp.stack([one, total - one])
    sizes = jnp.asarray(split_up(count, total, most, skew), jnp.int32)
    pairs = (count - 1) // 2
    giver, sink = sizes[1:1 + 2 * pairs:2], sizes[2:2 + 2 * pairs:2]
    slack = jnp.minimum(giver - 1, most - sink)
    passed = jax.random.randint(jax.random.fold_in(rng, 1), (pairs,), 0, 1 << 20) % (slack + 1)
    sizes = sizes.at[1:1 + 2 * pairs:2].set(giver - passed).at[2:2 + 2 * pairs:2].set(sink + passed)
    return sizes[jax.random.permutation(jax.random.fold_in(rng, 2), count)]


def noise(rng, shape, spread, limit, split=(), kind=jnp.bfloat16):
    entries = spread * jax.random.normal(rng, shape, jnp.float32)
    if split:
        entries = entries * steps_of(rng, shape, split, -0.22, 0.18)
    return jnp.clip(entries, -limit, limit).astype(kind)


def setup_inputs(seed: int = 0) -> dict:
    key_of = jax.random.split(jax.random.key(seed), 8)
    saved_inputs = noise(key_of[0], (SECTIONS, BUF, TOK_MB, D), 1.0, 6.0, ((0, 8), (2, 32)))
    slot_index = plant(jax.random.randint(key_of[1], (SECTIONS, SLOTS), 0, BUF), jax.random.fold_in(key_of[1], 1), 0, BUF - 1).astype(jnp.int32)
    example_lengths = jax.vmap(lambda own: uneven(own, EXAMPLES, TOK_MB, MOST, 2))(jax.random.split(key_of[2], SECTIONS * SLOTS)).reshape((SECTIONS, SLOTS, EXAMPLES)).astype(jnp.int32)
    first_grads = noise(key_of[3], (SECTIONS, TOK_MB, D), 1.0, 6.0, ((0, 8), (1, 32)))
    loss_grads = noise(key_of[4], (SLOTS - 1, TOK_MB, D), 1.0, 6.0, ((1, 32),))
    w_in = noise(key_of[5], (SECTIONS, D, FF), D ** -0.5, 0.1875, ((0, 8), (2, 32)))
    w_out = noise(key_of[6], (SECTIONS, FF, D), FF ** -0.5, 0.03125, ((0, 8), (1, 32)))
    return dict(saved_inputs=saved_inputs, slot_index=slot_index, example_lengths=example_lengths, first_grads=first_grads, loss_grads=loss_grads, w_in=w_in, w_out=w_out)


GAMMA = 0.01

def membership(lengths, tokens):
    ends = jnp.cumsum(lengths)
    position = jnp.arange(tokens, dtype=jnp.int32)
    example_id = lax.optimization_barrier(jnp.sum((position[:, None] >= ends[None, :-1]).astype(jnp.int32), axis=1))
    labels = jnp.arange(lengths.shape[0], dtype=jnp.int32)
    return (example_id[:, None] == labels[None, :]).astype(jnp.float32)

def section_step(inputs, grads, first, second, lengths):
    z = jnp.dot(inputs, first, preferred_element_type=jnp.float32)
    relu = jnp.maximum(z, 0.0)
    hidden = (relu * relu).astype(jnp.bfloat16)
    back = jnp.dot(grads, second.T, preferred_element_type=jnp.float32)
    dz = (2.0 * relu * back).astype(jnp.bfloat16)
    dx = (grads.astype(jnp.float32) + jnp.dot(dz, first.T, preferred_element_type=jnp.float32)).astype(jnp.bfloat16)
    member = membership(lengths, inputs.shape[0])
    gram_x = jnp.dot(inputs, inputs.T, preferred_element_type=jnp.float32)
    gram_z = jnp.dot(dz, dz.T, preferred_element_type=jnp.float32)
    gram_h = jnp.dot(hidden, hidden.T, preferred_element_type=jnp.float32)
    gram_y = jnp.dot(grads, grads.T, preferred_element_type=jnp.float32)
    paired = gram_x * gram_z + gram_h * gram_y
    squares = lax.optimization_barrier(jnp.sum(member * jnp.dot(paired, member, precision=lax.Precision.HIGHEST), axis=0))
    factor = 1.0 / (jnp.sqrt(squares / (D * FF)) + GAMMA)
    token_factor = lax.optimization_barrier(jnp.sum(member * factor[None, :], axis=1))
    dzc = (dz.astype(jnp.float32) * token_factor[:, None]).astype(jnp.bfloat16)
    dyc = (grads.astype(jnp.float32) * token_factor[:, None]).astype(jnp.bfloat16)
    g_first = jnp.dot(inputs.T, dzc, preferred_element_type=jnp.float32)
    g_second = jnp.dot(hidden.T, dyc, preferred_element_type=jnp.float32)
    return (dx, g_first, g_second)

def reference(saved_inputs, slot_index, example_lengths, first_grads, loss_grads, w_in, w_out):
    section_count = w_in.shape[0]
    slot_count = slot_index.shape[1]
    acc_first = [jnp.zeros((D, FF), jnp.float32) for s in range(section_count)]
    acc_second = [jnp.zeros((FF, D), jnp.float32) for s in range(section_count)]
    previous = [None] * section_count
    results = [[None] * slot_count for s in range(section_count)]
    for slot in range(slot_count):
        current = [None] * section_count
        for section in range(section_count):
            if slot == 0:
                grads = first_grads[section]
            elif section == section_count - 1:
                grads = loss_grads[slot - 1]
            else:
                grads = previous[section + 1]
            inputs = lax.dynamic_index_in_dim(saved_inputs[section], slot_index[section, slot].astype(jnp.int32), 0, keepdims=False)
            dx, g_first, g_second = section_step(inputs, grads, w_in[section], w_out[section], example_lengths[section, slot])
            acc_first[section] = acc_first[section] + g_first
            acc_second[section] = acc_second[section] + g_second
            current[section] = dx
            results[section][slot] = dx
        previous = current
    grad_in = jnp.stack(acc_first).astype(jnp.bfloat16)
    grad_out = jnp.stack(acc_second).astype(jnp.bfloat16)
    input_grads = jnp.stack([jnp.stack(row) for row in results])
    return (grad_in, grad_out, input_grads)
```

```python
import jax
import jax.numpy as jnp
from jax import lax
from jax.experimental import pallas as pl
from jax.experimental.pallas import tpu as pltpu
from jax.sharding import PartitionSpec as P

D = 1024
FF = 32768
GAMMA = 0.01
F32 = jnp.float32
BF16 = jnp.bfloat16
MIB = 1 << 20


def spread(shard):
    count = lax.axis_size("tensor")
    copies = jnp.broadcast_to(shard, (count, *shard.shape))
    arrived = lax.all_to_all(copies, "tensor", split_axis=0, concat_axis=0, tiled=True)
    return arrived.reshape(count * shard.shape[0], *shard.shape[1:])


def back_kernel(grads_ref, slope_ref, out_t_ref, in_t_ref, dz_ref, share_ref):
    hidden, width = in_t_ref.shape
    step = 256
    grads = grads_ref[...]
    for at in range(0, hidden, step):
        cols = slice(at, at + step)
        back = jnp.dot(grads, out_t_ref[:, cols], preferred_element_type=F32)
        dz_ref[:, cols] = (slope_ref[:, cols] * back).astype(BF16)
    dz = dz_ref[...]
    for at in range(0, width, step):
        cols = slice(at, at + step)
        share = jnp.dot(dz, in_t_ref[:, cols], preferred_element_type=F32)
        share_ref[:, cols] = share.astype(BF16)


def back_step(grads, slope, out_t, in_t):
    tokens, width = grads.shape
    hidden = in_t.shape[0]
    whole = pl.BlockSpec(memory_space=pltpu.VMEM)
    return pl.pallas_call(
        back_kernel,
        out_shape=(
            jax.ShapeDtypeStruct((tokens, hidden), BF16),
            jax.ShapeDtypeStruct((tokens, width), BF16),
        ),
        in_specs=[whole] * 4,
        out_specs=(whole, whole),
        compiler_params=pltpu.CompilerParams(vmem_limit_bytes=24 * MIB),
        cost_estimate=pl.CostEstimate(
            flops=4 * tokens * width * hidden, bytes_accessed=8 * MIB, transcendentals=0
        ),
    )(grads, slope, out_t, in_t)


def per_device(saved_inputs, slot_index, example_lengths, first_grads, loss_grads, w_in, w_out):
    sections = lax.axis_size("section")
    is_last = lax.axis_index("section") == sections - 1
    first, second = w_in[0], w_out[0]
    slots = loss_grads.shape[0] + 1
    picked = [
        lax.dynamic_index_in_dim(saved_inputs[0], slot_index[0, slot], 0, keepdims=False)
        for slot in range(slots)
    ]
    incoming = first_grads[0]
    start = spread(jnp.concatenate([picked[0], incoming], axis=1))
    out_t, in_t = second.T, first.T
    later, out_t, in_t = lax.optimization_barrier(
        (jnp.concatenate(picked[1:], axis=1), out_t, in_t)
    )
    later = spread(later)
    inputs = [start[:, :D]] + [later[:, D * i : D * (i + 1)] for i in range(slots - 1)]
    grads = start[:, D:]
    tokens = grads.shape[0]
    position = jnp.arange(tokens, dtype=jnp.int32)

    dzs, hiddens, dys, results, squares = [], [], [], [], []
    for slot in range(slots):
        x = inputs[slot]
        relu = jnp.maximum(jnp.dot(x, first, preferred_element_type=F32), 0.0)
        hidden = (relu * relu).astype(BF16)
        dz, share = back_step(grads, 2.0 * relu, out_t, in_t)
        arrived = lax.all_to_all(
            share.reshape(-1, 8, D), "tensor", split_axis=0, concat_axis=0, tiled=True
        )
        second_example = (position >= example_lengths[0, slot, 0]).astype(F32)
        same = second_example[:, None] == second_example[None, :]
        gram_x = jnp.einsum("td,ud->tu", x, x, preferred_element_type=F32)
        gram_z = jnp.einsum("tf,uf->tu", dz, dz, preferred_element_type=F32)
        gram_h = jnp.einsum("tf,uf->tu", hidden, hidden, preferred_element_type=F32)
        gram_y = jnp.einsum("td,ud->tu", grads, grads, preferred_element_type=F32)
        rows = jnp.sum(jnp.where(same, gram_x * gram_z + gram_h * gram_y, 0.0), axis=1)
        both = jnp.stack([1.0 - second_example, second_example])
        squares.append(jnp.sum(both * rows[None, :], axis=1))
        dzs.append(dz)
        hiddens.append(hidden)
        dys.append(grads)
        passing = (incoming.astype(F32) + jnp.sum(arrived.astype(F32), axis=0)).astype(BF16)
        results.append(passing)
        if slot + 1 < slots:
            shifted = lax.ppermute(
                passing, "section", [(source, source - 1) for source in range(1, sections)]
            )
            incoming = jnp.where(is_last, loss_grads[slot], shifted)
            grads = spread(incoming)

    mine = jnp.concatenate(squares)
    mine = jnp.pad(mine, (0, 128 - mine.shape[0]))[None]
    totals = jnp.sum(spread(mine), axis=0)[: 2 * slots].reshape(slots, 2)
    factor = 1.0 / (jnp.sqrt(totals / (D * FF)) + GAMMA)
    scale = jnp.concatenate(
        [
            jnp.where(position >= example_lengths[0, slot, 0], factor[slot, 1], factor[slot, 0])
            for slot in range(slots)
        ]
    )[:, None]
    dzc = (jnp.concatenate(dzs).astype(F32) * scale).astype(BF16)
    dyc = (jnp.concatenate(dys).astype(F32) * scale).astype(BF16)
    grad_in = jnp.einsum(
        "td,tf->df", jnp.concatenate(inputs), dzc, preferred_element_type=F32
    ).astype(BF16)
    grad_out = jnp.einsum(
        "tf,td->fd", jnp.concatenate(hiddens), dyc, preferred_element_type=F32
    ).astype(BF16)
    return grad_in[None], grad_out[None], jnp.stack(results)[None]


def solution(mesh):
    return jax.shard_map(
        per_device,
        mesh=mesh,
        in_specs=(
            P("section", None, "tensor", None),
            P("section", None),
            P("section", None, None),
            P("section", "tensor", None),
            P(None, "tensor", None),
            P("section", None, "tensor"),
            P("section", "tensor", None),
        ),
        out_specs=(
            P("section", None, "tensor"),
            P("section", "tensor", None),
            P("section", None, "tensor", None),
        ),
        check_vma=False,
    )
```

```python
import jax
import jax.numpy as jnp
from jax import lax
from jax.experimental import pallas as pl
from jax.experimental.pallas import tpu as pltpu
from jax.sharding import PartitionSpec as P

D = 1024
FF = 32768
GAMMA = 0.01
F32 = jnp.float32
BF16 = jnp.bfloat16
MIB = 1 << 20
STEP = 256
LANES = 128

ANY = pl.BlockSpec(memory_space=pl.ANY)
SMEM = pl.BlockSpec(memory_space=pltpu.SMEM)


def shape(*dims, dtype=BF16):
    return jax.ShapeDtypeStruct(dims, dtype)


def call(kernel, outs, operands, scratch, copies, flops, name, smem=0):
    return pl.pallas_call(
        kernel,
        out_shape=outs,
        in_specs=[SMEM] * smem + [ANY] * (len(operands) - smem),
        out_specs=jax.tree.map(lambda _: ANY, outs),
        scratch_shapes=[pltpu.VMEM(dims, dtype) for dims, dtype in scratch]
        + [pltpu.SemaphoreType.DMA((copies,))],
        name=name,
        compiler_params=pltpu.CompilerParams(vmem_limit_bytes=60 * MIB),
        cost_estimate=pl.CostEstimate(flops=flops, bytes_accessed=4 * MIB, transcendentals=0),
    )(*operands)


class Copies:
    def __init__(self, sems):
        self.sems, self.used, self.open = sems, 0, []

    def start(self, source, target):
        copy = pltpu.make_async_copy(source, target, self.sems.at[self.used])
        self.used += 1
        copy.start()
        return copy

    def store(self, source, target):
        self.open.append(self.start(source, target))

    def finish(self):
        for copy in self.open:
            copy.wait()


def parts(extent):
    return [slice(at, at + STEP) for at in range(0, extent, STEP)]


def nt(a, b):
    return lax.dot_general(a, b, (((1,), (1,)), ((), ())), preferred_element_type=F32)


def mm(a, b):
    return jnp.dot(a, b, preferred_element_type=F32)


def start_kernel(index, saved, grads, blocks, saved_v, row_v, sems):
    copies = Copies(sems)
    loads = [copies.start(saved, saved_v), copies.start(grads, row_v.at[:, D:])]
    for load in loads:
        load.wait()
    row_v[:, :D] = saved_v[index[0, 0]]
    for peer in range(blocks.shape[0]):
        copies.store(row_v, blocks.at[peer])
    copies.finish()


def spread_kernel(last, shifted, loss, blocks, chosen, shifted_v, loss_v, sems):
    copies = Copies(sems)
    loads = [copies.start(shifted, shifted_v), copies.start(loss, loss_v)]
    for load in loads:
        load.wait()
    shifted_v[...] = jnp.where(last[0] > 0, loss_v[...], shifted_v[...])
    for peer in range(blocks.shape[0]):
        copies.store(shifted_v, blocks.at[peer])
    copies.store(shifted_v, chosen)
    copies.finish()


def picked(place, index, source):
    if len(source.shape) == 2:
        return source.at[:, :D]
    return source.at[index[0, place]]


def forward_kernel(place, index, source, weights, slope, hidden, x_v, w_v, slope_v, hidden_v, sems):
    copies = Copies(sems)
    x_load = copies.start(picked(place, index, source), x_v)
    chunks = parts(weights.shape[1])
    loads = [copies.start(weights.at[:, cols], w_v.at[:, cols]) for cols in chunks]
    x_load.wait()
    for cols, load in zip(chunks, loads):
        load.wait()
        relu = jnp.maximum(mm(x_v[...], w_v[:, cols]), 0.0)
        slope_v[:, cols] = 2.0 * relu
        hidden_v[:, cols] = (relu * relu).astype(BF16)
        copies.store(slope_v.at[:, cols], slope.at[:, cols])
        copies.store(hidden_v.at[:, cols], hidden.at[:, cols])
    copies.finish()


def masked_sums(slot, lengths, paired):
    cut = lengths[0, 2 * slot]
    tokens = paired.shape[0]
    row = lax.broadcasted_iota(jnp.int32, (tokens, tokens), 0) < cut
    col = lax.broadcasted_iota(jnp.int32, (tokens, tokens), 1) < cut
    before = jnp.sum(jnp.where(row & col, paired, 0.0), axis=(0, 1), keepdims=True)
    after = jnp.sum(jnp.where(row | col, 0.0, paired), axis=(0, 1), keepdims=True)
    lane = lax.broadcasted_iota(jnp.int32, (1, LANES), 1)
    return jnp.where(lane == 2 * slot, before, jnp.where(lane == 2 * slot + 1, after, 0.0))


def back_kernel(
    col, slot, lengths, source, slope, w_out, w_in, *refs
):
    if slot is None:
        dz, share, g_v, slope_v, out_v, in_v, dz_v, share_v, sems = refs
    else:
        gram_x, gram_h, sums = refs[:3]
        dz, share, g_v, slope_v, out_v, in_v, dz_v, share_v, gx_v, gh_v, sums_v, sems = refs[3:]
    copies = Copies(sems)
    g_load = copies.start(source.at[:, col : col + D], g_v)
    hidden_parts, model_parts = parts(w_out.shape[0]), parts(w_in.shape[0])
    firsts = [
        (
            copies.start(w_out.at[part, :], out_v.at[part, :]),
            copies.start(slope.at[:, part], slope_v.at[:, part]),
        )
        for part in hidden_parts
    ]
    seconds = [copies.start(w_in.at[part, :], in_v.at[part, :]) for part in model_parts]
    if slot is not None:
        extra = [
            copies.start(a, b) for a, b in ((gram_x, gx_v), (gram_h, gh_v), (sums, sums_v))
        ]
    g_load.wait()
    for part, loads in zip(hidden_parts, firsts):
        for load in loads:
            load.wait()
        back = nt(g_v[...], out_v[part, :])
        dz_v[:, part] = (slope_v[:, part] * back).astype(BF16)
        copies.store(dz_v.at[:, part], dz.at[:, part])
    for part, load in zip(model_parts, seconds):
        load.wait()
        share_v[:, part] = nt(dz_v[...], in_v[part, :]).astype(BF16)
        copies.store(share_v.at[:, part], share.at[:, part])
    if slot is not None:
        for load in extra:
            load.wait()
        paired = gx_v[...] * nt(dz_v[...], dz_v[...]) + gh_v[...] * nt(g_v[...], g_v[...])
        total = sums_v[...] + masked_sums(slot, lengths, paired)
        high = total.astype(BF16)
        rest = total - high.astype(F32)
        middle = rest.astype(BF16)
        low = (rest - middle.astype(F32)).astype(BF16)
        lane = lax.broadcasted_iota(jnp.int32, (1, LANES), 1)
        line = jnp.zeros((1, LANES), F32)
        for place, piece in enumerate((high, middle, low)):
            line = line + pltpu.roll(piece.astype(F32), place * SPACING, 1)
        tokens = share_v.shape[0]
        share_v[:, D:] = jnp.broadcast_to(line, (tokens, LANES)).astype(BF16)
        copies.store(share_v.at[:, D:], share.at[:, D:])
    copies.finish()


SPACING = 32


def shadow_kernel(
    g_col, slot, lengths, index, x, hidden, grads, dz, x_t, hidden_t, sums,
    x_v, hidden_v, g_v, dz_v, xt_v, ht_v, sums_v, sems,
):
    copies = Copies(sems)
    pairs = (
        (picked(slot, index, x), x_v),
        (hidden, hidden_v),
        (grads.at[:, g_col : g_col + D], g_v),
        (dz, dz_v),
    )
    for load in [copies.start(a, b) for a, b in pairs]:
        load.wait()
    xt_v[...] = x_v[...].T
    copies.store(xt_v, x_t)
    ht_v[...] = hidden_v[...].T
    copies.store(ht_v, hidden_t)
    paired = nt(x_v[...], x_v[...]) * nt(dz_v[...], dz_v[...])
    paired = paired + nt(hidden_v[...], hidden_v[...]) * nt(g_v[...], g_v[...])
    sums_v[...] = masked_sums(slot, lengths, paired)
    copies.store(sums_v, sums)
    copies.finish()


def grams_kernel(
    place, index, x, hidden, x_t, hidden_t, gram_x, gram_h, x_v, hidden_v, xt_v, ht_v, gx_v, gh_v, sems
):
    copies = Copies(sems)
    for load in [copies.start(picked(place, index, x), x_v), copies.start(hidden, hidden_v)]:
        load.wait()
    xt_v[...] = x_v[...].T
    copies.store(xt_v, x_t)
    ht_v[...] = hidden_v[...].T
    copies.store(ht_v, hidden_t)
    gx_v[...] = nt(x_v[...], x_v[...])
    copies.store(gx_v, gram_x)
    gh_v[...] = nt(hidden_v[...], hidden_v[...])
    copies.store(gh_v, gram_h)
    copies.finish()


def sum_kernel(arrived_ref, incoming_ref, *out_refs):
    total = jnp.sum(arrived_ref[:, :, :D].astype(F32), axis=0)
    out_refs[0][...] = (incoming_ref[...].astype(F32) + total).astype(BF16)
    if len(out_refs) > 1:
        line = jnp.sum(arrived_ref[:, 0:1, D:].astype(F32), axis=0)
        back = [pltpu.roll(line, LANES - place * SPACING, 1) for place in (1, 2)]
        out_refs[1][...] = line + (back[0] + back[1])


def add_up(arrived, incoming, with_sums):
    outs = [shape(*incoming.shape)] + ([shape(1, LANES, dtype=F32)] if with_sums else [])
    whole = pl.BlockSpec(memory_space=pltpu.VMEM)
    return pl.pallas_call(
        sum_kernel,
        out_shape=outs,
        in_specs=[whole] * 2,
        out_specs=[whole] * len(outs),
        name="add_up",
        compiler_params=pltpu.CompilerParams(vmem_limit_bytes=60 * MIB),
        cost_estimate=pl.CostEstimate(flops=arrived.size, bytes_accessed=MIB, transcendentals=0),
    )(arrived, incoming)


def final_kernel(slots, lengths_ref, totals_ref, *refs):
    x_t, hidden_t, dz, dy = (refs[i * slots : (i + 1) * slots] for i in range(4))
    grad_in_ref, grad_out_ref, dzc_ref, dyc_ref = refs[4 * slots :]

    @pl.when(pl.program_id(0) == 0)
    def _():
        factor = 1.0 / (jnp.sqrt(totals_ref[...] / (D * FF)) + GAMMA)
        for slot in range(slots):
            tokens = dz[slot].shape[0]
            row = lax.broadcasted_iota(jnp.int32, (tokens, 1), 0) < lengths_ref[0, 2 * slot]
            scale = jnp.where(
                row,
                factor[:, 2 * slot : 2 * slot + 1],
                factor[:, 2 * slot + 1 : 2 * slot + 2],
            )
            rows = slice(slot * tokens, (slot + 1) * tokens)
            dzc_ref[rows, :] = (dz[slot][...].astype(F32) * scale).astype(BF16)
            dyc_ref[rows, :] = (dy[slot][...].astype(F32) * scale).astype(BF16)

    for left, right_ref, out_ref in ((x_t, dzc_ref, grad_in_ref), (hidden_t, dyc_ref, grad_out_ref)):
        lhs = jnp.concatenate([part[...] for part in left], axis=1)
        for cols in parts(right_ref.shape[1]):
            out_ref[:, cols] = mm(lhs, right_ref[:, cols]).astype(BF16)


def final_products(lengths, totals, x_t, hidden_t, dz, dy):
    slots = len(dz)
    rows, tokens = x_t[0].shape
    width = dz[0].shape[1]
    block = 256
    strip = pl.BlockSpec((block, tokens), lambda i: (i, 0))
    whole = pl.BlockSpec((tokens, width), lambda i: (0, 0), pipeline_mode=pl.Buffered(1))
    dy_specs = [
        pl.BlockSpec((tokens, D), lambda i, at=col // D: (0, at), pipeline_mode=pl.Buffered(1))
        for _, col in dy
    ]
    out = pl.BlockSpec((block, width), lambda i: (i, 0))
    return pl.pallas_call(
        lambda *refs: final_kernel(slots, *refs),
        grid=(rows // block,),
        out_shape=(shape(rows, width), shape(rows, width)),
        in_specs=[SMEM, pl.BlockSpec(totals.shape, lambda i: (0, 0))]
        + [strip] * (2 * slots)
        + [whole] * slots
        + dy_specs,
        out_specs=(out, out),
        scratch_shapes=[pltpu.VMEM((slots * tokens, width), BF16)] * 2,
        name="final",
        compiler_params=pltpu.CompilerParams(vmem_limit_bytes=60 * MIB),
        cost_estimate=pl.CostEstimate(
            flops=4 * rows * width * slots * tokens, bytes_accessed=10 * MIB, transcendentals=0
        ),
    )(lengths, totals, *x_t, *hidden_t, *dz, *[array for array, _ in dy])


def exchange(blocks):
    return lax.all_to_all(blocks, "tensor", split_axis=0, concat_axis=0, tiled=True)


def per_device(saved_inputs, slot_index, example_lengths, first_grads, loss_grads, w_in, w_out):
    sections, count = lax.axis_size("section"), lax.axis_size("tensor")
    is_last = (lax.axis_index("section") == sections - 1).astype(jnp.int32).reshape(1)
    first, second = w_in[0], w_out[0]
    slots = loss_grads.shape[0] + 1
    rows = first_grads.shape[1]
    tokens = count * rows
    units = first.shape[1]
    lengths = example_lengths.reshape(1, 2 * slots)
    incoming = first_grads[0]
    product = 2 * tokens * D * units
    wide = (tokens, D)

    later = lax.all_gather(saved_inputs[0], "tensor", axis=1, tiled=True)
    blocks = call(
        start_kernel,
        shape(count, rows, 2 * D),
        (slot_index, saved_inputs[0], incoming),
        [(saved_inputs.shape[1:], BF16), ((rows, 2 * D), BF16)],
        count + 2,
        0,
        "start",
        smem=1,
    )
    begun = exchange(blocks).reshape(tokens, 2 * D)
    inputs = [begun] + [later] * (slots - 1)
    grads = (begun, D)

    x_t, hidden_t, dzs, dys, results = [], [], [], [], []
    sums = jnp.zeros((1, LANES), F32)
    for slot in range(slots):
        final = slot + 1 == slots
        x = inputs[slot]
        g, g_col = grads
        slope, hidden = call(
            lambda *refs, slot=slot: forward_kernel(slot, *refs),
            (shape(tokens, units, dtype=F32), shape(tokens, units)),
            (slot_index, x, first),
            [(wide, BF16), (first.shape, BF16), ((tokens, units), F32), ((tokens, units), BF16)],
            1 + 3 * (units // STEP),
            product,
            "forward",
            smem=1,
        )
        flipped = (shape(D, tokens), shape(units, tokens))
        flipped_v = [((D, tokens), BF16), ((units, tokens), BF16)]
        square = (tokens, tokens)
        width = D + (LANES if final else 0)
        extra, extra_v = (), []
        if final:
            *turned, gram_x, gram_h = call(
                lambda *refs, slot=slot: grams_kernel(slot, *refs),
                flipped + (shape(*square, dtype=F32),) * 2,
                (slot_index, x, hidden),
                [(wide, BF16), ((tokens, units), BF16)] + flipped_v + [(square, F32)] * 2,
                6,
                product,
                "grams",
                smem=1,
            )
            extra, extra_v = (gram_x, gram_h, sums), [(square, F32)] * 2 + [((1, LANES), F32)]
        dz, share = call(
            lambda *refs, col=g_col, slot=slot if final else None: back_kernel(col, slot, *refs),
            (shape(tokens, units), shape(tokens, width)),
            (lengths, g, slope, second, first, *extra),
            [
                (wide, BF16),
                ((tokens, units), F32),
                (second.shape, BF16),
                (first.shape, BF16),
                ((tokens, units), BF16),
                ((tokens, width), BF16),
            ]
            + extra_v,
            1 + 3 * (units // STEP) + 2 * (D // STEP) + 4,
            2 * product,
            "back",
            smem=1,
        )
        arrived = exchange(share.reshape(count, rows, width))
        if not final:
            *turned, one = call(
                lambda *refs, col=g_col, slot=slot: shadow_kernel(col, slot, *refs),
                flipped + (shape(1, LANES, dtype=F32),),
                (lengths, slot_index, x, hidden, g, dz),
                [(wide, BF16), ((tokens, units), BF16), (wide, BF16), ((tokens, units), BF16)]
                + flipped_v
                + [((1, LANES), F32)],
                7,
                product,
                "shadow",
                smem=2,
            )
            sums = sums + one
        x_t.append(turned[0])
        hidden_t.append(turned[1])
        dzs.append(dz)
        dys.append(grads)
        passing, *totals = add_up(arrived, incoming, final)
        results.append(passing)
        if not final:
            shifted = lax.ppermute(
                passing, "section", [(source, source - 1) for source in range(1, sections)]
            )
            blocks, incoming = call(
                spread_kernel,
                (shape(count, rows, D), shape(rows, D)),
                (is_last, shifted, loss_grads[slot]),
                [((rows, D), BF16)] * 2,
                count + 3,
                0,
                "spread",
                smem=1,
            )
            grads = (exchange(blocks).reshape(tokens, D), 0)

    grad_in, grad_out = final_products(lengths, totals[0], x_t, hidden_t, dzs, dys)
    return grad_in[None], grad_out[None], jnp.stack(results)[None]


def solution(mesh):
    return jax.shard_map(
        per_device,
        mesh=mesh,
        in_specs=(
            P("section", None, "tensor", None),
            P("section", None),
            P("section", None, None),
            P("section", "tensor", None),
            P(None, "tensor", None),
            P("section", None, "tensor"),
            P("section", "tensor", None),
        ),
        out_specs=(
            P("section", None, "tensor"),
            P("section", "tensor", None),
            P("section", None, "tensor", None),
        ),
        check_vma=False,
    )
```

```python
import jax
import jax.numpy as jnp
from jax import lax
from jax.experimental import pallas as pl
from jax.experimental.pallas import tpu as pltpu
from jax.sharding import PartitionSpec as P

D = 1024
FF = 32768
GAMMA = 0.01
F32 = jnp.float32
BF16 = jnp.bfloat16
MIB = 1 << 20
STEP = 256
LANES = 128
SPACING = 32

VMEM = pl.BlockSpec(memory_space=pltpu.VMEM)


def shape(*dims, dtype=BF16):
    return jax.ShapeDtypeStruct(dims, dtype)


def call(kernel, outs, operands, flops, name):
    return pl.pallas_call(
        kernel,
        out_shape=outs,
        in_specs=[VMEM] * len(operands),
        out_specs=jax.tree.map(lambda _: VMEM, outs),
        name=name,
        compiler_params=pltpu.CompilerParams(vmem_limit_bytes=8 * MIB),
        cost_estimate=pl.CostEstimate(flops=flops, bytes_accessed=MIB, transcendentals=0),
    )(*operands)


def parts(extent):
    return [slice(at, at + STEP) for at in range(0, extent, STEP)]


def nt(a, b):
    return lax.dot_general(a, b, (((1,), (1,)), ((), ())), preferred_element_type=F32)


def tn(a, b):
    return lax.dot_general(a, b, (((0,), (0,)), ((), ())), preferred_element_type=F32)


def mm(a, b):
    return jnp.dot(a, b, preferred_element_type=F32)


def start_kernel(index_ref, saved_ref, grads_ref, blocks_ref, *later_refs):
    count, rows, _ = blocks_ref.shape
    for slot in range(len(later_refs) + 1):
        wanted = index_ref[:, slot : slot + 1]
        x = saved_ref[0]
        for place in range(1, saved_ref.shape[0]):
            x = jnp.where(wanted == place, saved_ref[place], x)
        if slot:
            later_refs[slot - 1][...] = x
        else:
            blocks_ref[:, :, :D] = jnp.broadcast_to(x[None], (count, rows, D))
    blocks_ref[:, :, D:] = jnp.broadcast_to(grads_ref[...][None], (count, rows, D))


def spread_kernel(sections, place, shifted_ref, loss_ref, blocks_ref, rows_ref):
    last = (lax.axis_index("section") == sections - 1).astype(jnp.int32)
    chosen = jnp.where(jnp.full(rows_ref.shape, last) > 0, loss_ref[place], shifted_ref[...])
    rows_ref[...] = chosen
    blocks_ref[...] = jnp.broadcast_to(chosen[None], blocks_ref.shape)


def forward_kernel(x_ref, weights_ref, slope_ref, hidden_ref):
    x = x_ref[:, :, -D:].reshape(-1, D) if len(x_ref.shape) == 3 else x_ref[...]
    for cols in parts(weights_ref.shape[1]):
        relu = jnp.maximum(mm(x, weights_ref[:, cols]), 0.0)
        slope_ref[:, cols] = 2.0 * relu
        hidden_ref[:, cols] = (relu * relu).astype(BF16)


def masked_sums(slot, lengths_ref, paired):
    cut = lengths_ref[0:1, slot : slot + 1]
    tokens = paired.shape[0]
    row = lax.broadcasted_iota(jnp.int32, (tokens, tokens), 0) < cut
    col = lax.broadcasted_iota(jnp.int32, (tokens, tokens), 1) < cut
    before = jnp.sum(jnp.where(row & col, paired, 0.0), axis=(0, 1), keepdims=True)
    after = jnp.sum(jnp.where(row | col, 0.0, paired), axis=(0, 1), keepdims=True)
    lane = lax.broadcasted_iota(jnp.int32, (1, LANES), 1)
    return jnp.where(lane == 2 * slot, before, jnp.where(lane == 2 * slot + 1, after, 0.0))


def back_products(grads, slope_ref, w_out_ref, w_in_ref, dz_ref, share_ref):
    for part in parts(w_out_ref.shape[0]):
        back = nt(grads, w_out_ref[part, :])
        dz_ref[:, part] = (slope_ref[:, part] * back).astype(BF16)
    dz = dz_ref[...]
    for part in parts(w_in_ref.shape[0]):
        share_ref[:, part] = nt(dz, w_in_ref[part, :]).astype(BF16)
    return dz


def back_kernel(grads_ref, slope_ref, w_out_ref, w_in_ref, riding_ref, dz_ref, share_ref):
    back_products(grads_ref[...], slope_ref, w_out_ref, w_in_ref, dz_ref, share_ref)
    copies = share_ref.shape[0] // riding_ref.shape[0]
    share_ref[:, D:] = jnp.concatenate([riding_ref[...]] * copies, axis=0)


def last_back_kernel(
    slot, lengths_ref, grads_ref, slope_ref, w_out_ref, w_in_ref, gram_x_ref, gram_h_ref, *refs
):
    *sums_refs, dz_ref, share_ref = refs
    grads = grads_ref[...]
    dz = back_products(grads, slope_ref, w_out_ref, w_in_ref, dz_ref, share_ref)
    paired = gram_x_ref[...] * nt(dz, dz) + gram_h_ref[...] * nt(grads, grads)
    total = masked_sums(slot, lengths_ref, paired)
    for sums_ref in sums_refs:
        total = total + sums_ref[...]
    high = total.astype(BF16)
    rest = total - high.astype(F32)
    middle = rest.astype(BF16)
    low = (rest - middle.astype(F32)).astype(BF16)
    line = high.astype(F32)
    for place, piece in ((1, middle), (2, low)):
        line = line + pltpu.roll(piece.astype(F32), place * SPACING, 1)
    share_ref[:, D:] = jnp.broadcast_to(line, (share_ref.shape[0], LANES)).astype(BF16)


def squares_kernel(slot, lengths_ref, x_ref, hidden_ref, grads_ref, dz_ref, sums_ref):
    x, hidden, grads, dz = x_ref[...], hidden_ref[...], grads_ref[...], dz_ref[...]
    paired = nt(x, x) * nt(dz, dz) + nt(hidden, hidden) * nt(grads, grads)
    sums_ref[...] = masked_sums(slot, lengths_ref, paired)


def grams_kernel(x_ref, hidden_ref, gram_x_ref, gram_h_ref):
    x, hidden = x_ref[...], hidden_ref[...]
    gram_x_ref[...] = nt(x, x)
    gram_h_ref[...] = nt(hidden, hidden)


def sum_kernel(arrived_ref, incoming_ref, passing_ref, x_ref):
    total = incoming_ref[...].astype(F32)
    for peer in range(arrived_ref.shape[0]):
        total = total + arrived_ref[peer, :, :D].astype(F32)
    passing_ref[...] = total.astype(BF16)
    x_ref[...] = arrived_ref[:, :, D:].reshape(x_ref.shape)


def last_sum_kernel(arrived_ref, incoming_ref, *refs):
    *earlier_refs, results_ref, line_ref = refs
    total = incoming_ref[...].astype(F32)
    line = jnp.zeros(line_ref.shape, F32)
    for peer in range(arrived_ref.shape[0]):
        total = total + arrived_ref[peer, :, :D].astype(F32)
        line = line + arrived_ref[peer, 0:1, D:].astype(F32)
    for place, earlier_ref in enumerate(earlier_refs):
        results_ref[place] = earlier_ref[...]
    results_ref[len(earlier_refs)] = total.astype(BF16)
    pieces = [pltpu.roll(line, LANES - place * SPACING, 1) for place in (1, 2)]
    line_ref[...] = line + (pieces[0] + pieces[1])


def final_kernel(slots, lengths_ref, totals_ref, *refs):
    x, hidden, dz, dy = (refs[i * slots : (i + 1) * slots] for i in range(4))
    grad_in_ref, grad_out_ref, dzc_ref, dyc_ref = refs[4 * slots :]
    tokens = dz[0].shape[0]
    step = pl.program_id(0)

    @pl.when(step == 0)
    def _():
        factor = 1.0 / (jnp.sqrt(totals_ref[...] / (D * FF)) + GAMMA)
        for slot in range(slots):
            cut = lengths_ref[0:1, slot : slot + 1]
            row = lax.broadcasted_iota(jnp.int32, (tokens, 1), 0) < cut
            scale = jnp.where(
                row,
                factor[:, 2 * slot : 2 * slot + 1],
                factor[:, 2 * slot + 1 : 2 * slot + 2],
            )
            rows = slice(slot * tokens, (slot + 1) * tokens)
            dzc_ref[rows, :] = (dz[slot][...].astype(F32) * scale).astype(BF16)
            dyc_ref[rows, :] = (dy[slot][...].astype(F32) * scale).astype(BF16)

    block = grad_in_ref.shape[0]
    strip = pl.ds(pl.multiple_of(step * block, block), block)
    for left, right_ref, out_ref in ((x, dzc_ref, grad_in_ref), (hidden, dyc_ref, grad_out_ref)):
        for cols in parts(right_ref.shape[1]):
            total = tn(left[0][:, strip], right_ref[:tokens, cols])
            for slot in range(1, slots):
                rows = slice(slot * tokens, (slot + 1) * tokens)
                total = total + tn(left[slot][:, strip], right_ref[rows, cols])
            out_ref[:, cols] = total.astype(BF16)


def final_products(lengths, totals, x, hidden, dz, dy):
    slots = len(dz)
    tokens, width = dz[0].shape
    rows = x[0].shape[1]
    block = 256
    out = pl.BlockSpec((block, width), lambda i: (i, 0))
    return pl.pallas_call(
        lambda *refs: final_kernel(slots, *refs),
        grid=(rows // block,),
        out_shape=(shape(rows, width), shape(rows, width)),
        in_specs=[VMEM] * (2 + 4 * slots),
        out_specs=(out, out),
        scratch_shapes=[pltpu.VMEM((slots * tokens, width), BF16)] * 2,
        name="final",
        compiler_params=pltpu.CompilerParams(vmem_limit_bytes=12 * MIB),
        cost_estimate=pl.CostEstimate(
            flops=4 * rows * width * slots * tokens, bytes_accessed=4 * MIB, transcendentals=0
        ),
    )(lengths, totals, *x, *hidden, *dz, *dy)


def exchange(blocks):
    return lax.all_to_all(blocks, "tensor", split_axis=0, concat_axis=0, tiled=True)


def split_kernel(begun_ref, x_ref, grads_ref):
    x_ref[...] = begun_ref[:, :, :D].reshape(x_ref.shape)
    grads_ref[...] = begun_ref[:, :, D:].reshape(grads_ref.shape)


def per_device(saved_inputs, slot_index, example_lengths, first_grads, loss_grads, w_in, w_out):
    sections, count = lax.axis_size("section"), lax.axis_size("tensor")
    first, second = w_in[0], w_out[0]
    slots = loss_grads.shape[0] + 1
    rows = first_grads.shape[1]
    tokens = count * rows
    units = first.shape[1]
    lengths = example_lengths[0].T
    incoming = first_grads[0]
    product = 2 * tokens * D * units
    square = (tokens, tokens)

    blocks, *riding = call(
        start_kernel,
        (shape(count, rows, 2 * D),) + (shape(rows, D),) * (slots - 1),
        (slot_index, saved_inputs[0], incoming),
        0,
        "start",
    )
    begun = exchange(blocks)
    x, grads = call(split_kernel, (shape(tokens, D),) * 2, (begun,), 0, "split")

    def forward(x):
        outs = (shape(tokens, units, dtype=F32), shape(tokens, units))
        return call(forward_kernel, outs, (x, first), product, "forward")

    slope, hidden = forward(x)
    xs, hiddens, dzs, dys, results, squares = [], [], [], [], [], []
    for slot in range(slots):
        xs.append(x)
        hiddens.append(hidden)
        dys.append(grads)
        if slot + 1 == slots:
            break
        dz, share = call(
            back_kernel,
            (shape(tokens, units), shape(tokens, 2 * D)),
            (grads, slope, second, first, riding[slot]),
            2 * product,
            "back",
        )
        dzs.append(dz)
        arrived = exchange(share.reshape(count, rows, 2 * D))
        passing, next_x = call(
            sum_kernel,
            (shape(rows, D), shape(tokens, D)),
            (arrived, incoming),
            tokens * D,
            "add_up",
        )
        results.append(passing)
        shifted = lax.ppermute(
            passing, "section", [(source, source - 1) for source in range(1, sections)]
        )
        held = lax.optimization_barrier((passing, x, hidden, grads, dz))
        one = call(
            lambda *refs, slot=slot: squares_kernel(slot, *refs),
            shape(1, LANES, dtype=F32),
            (lengths, *held[1:]),
            product,
            "squares",
        )
        squares.append(one)
        x = next_x
        slope, hidden = forward(x)
        ready = [one, slope, hidden]
        if slot + 2 == slots:
            ready += call(
                grams_kernel, (shape(*square, dtype=F32),) * 2, (x, hidden), product // 4, "grams"
            )
        shifted, squares[-1], slope, hidden, *grams = lax.optimization_barrier((shifted, *ready))
        blocks, incoming = call(
            lambda *refs, slot=slot: spread_kernel(sections, slot, *refs),
            (shape(count, rows, D), shape(rows, D)),
            (shifted, loss_grads),
            0,
            "spread",
        )
        grads = exchange(blocks).reshape(tokens, D)

    dz, share = call(
        lambda *refs: last_back_kernel(slots - 1, *refs),
        (shape(tokens, units), shape(tokens, D + LANES)),
        (lengths, grads, slope, second, first, *grams, *squares),
        2 * product,
        "last_back",
    )
    dzs.append(dz)
    arrived = exchange(share.reshape(count, rows, D + LANES))
    results, totals = call(
        last_sum_kernel,
        (shape(slots, rows, D), shape(1, LANES, dtype=F32)),
        (arrived, incoming, *results),
        tokens * D,
        "last_add_up",
    )
    grad_in, grad_out = final_products(lengths, totals, xs, hiddens, dzs, dys)
    return grad_in[None], grad_out[None], results[None]


def solution(mesh):
    return jax.shard_map(
        per_device,
        mesh=mesh,
        in_specs=(
            P("section", None, "tensor", None),
            P("section", None),
            P("section", None, None),
            P("section", "tensor", None),
            P(None, "tensor", None),
            P("section", None, "tensor"),
            P("section", "tensor", None),
        ),
        out_specs=(
            P("section", None, "tensor"),
            P("section", "tensor", None),
            P("section", None, "tensor", None),
        ),
        check_vma=False,
    )
```

```python
import jax
import jax.numpy as jnp
from jax import lax
from jax.experimental import pallas as pl
from jax.experimental.pallas import tpu as pltpu
from jax.sharding import PartitionSpec as P

D = 1024
FF = 32768
GAMMA = 0.01
F32 = jnp.float32
BF16 = jnp.bfloat16
MIB = 1 << 20
STEP = 256
LANES = 128
SPACING = 32
ALONG_X = 4

VMEM = pl.BlockSpec(memory_space=pltpu.VMEM)


def shape(*dims, dtype=BF16):
    return jax.ShapeDtypeStruct(dims, dtype)


def call(kernel, outs, operands, flops, name):
    return pl.pallas_call(
        kernel,
        out_shape=outs,
        in_specs=[VMEM] * len(operands),
        out_specs=jax.tree.map(lambda _: VMEM, outs),
        name=name,
        compiler_params=pltpu.CompilerParams(vmem_limit_bytes=8 * MIB),
        cost_estimate=pl.CostEstimate(flops=flops, bytes_accessed=MIB, transcendentals=0),
    )(*operands)


def parts(extent):
    return [slice(at, at + STEP) for at in range(0, extent, STEP)]


def nt(a, b):
    return lax.dot_general(a, b, (((1,), (1,)), ((), ())), preferred_element_type=F32)


def tn(a, b):
    return lax.dot_general(a, b, (((0,), (0,)), ((), ())), preferred_element_type=F32)


def mm(a, b):
    return jnp.dot(a, b, preferred_element_type=F32)


def start_kernel(index, saved, grads, blocks_ref, index_v, saved_v, grads_v, sems):
    loads = [
        pltpu.make_async_copy(source, target, sems.at[place])
        for place, (source, target) in enumerate(
            ((index, index_v), (saved, saved_v), (grads, grads_v))
        )
    ]
    for load in loads:
        load.start()
    for load in loads:
        load.wait()
    count, rows, width = blocks_ref.shape
    for slot in range(index_v.shape[1]):
        wanted = index_v[:, slot : slot + 1]
        x = saved_v[0]
        for place in range(1, saved_v.shape[0]):
            x = jnp.where(wanted == place, saved_v[place], x)
        at = slot + 1 if slot else 0
        blocks_ref[:, :, D * at : D * (at + 1)] = jnp.broadcast_to(x[None], (count, rows, D))
    blocks_ref[:, :, D : 2 * D] = jnp.broadcast_to(grads_v[...][None], (count, rows, D))


def split_kernel(begun_ref, *out_refs):
    width = out_refs[0].shape[-1]
    for place, out_ref in enumerate(out_refs):
        out_ref[...] = begun_ref[:, :, width * place : width * (place + 1)]


def assemble_kernel(*refs):
    blocks, out_refs = refs[:ALONG_X], refs[ALONG_X:]
    mine = lax.axis_index("tensor") % ALONG_X
    for distance, block_ref in enumerate(blocks):
        source = (mine + (ALONG_X - distance)) % ALONG_X
        for place, out_ref in enumerate(out_refs):
            out_ref[:, pl.ds(source, 1)] = block_ref[:, :, D * place : D * (place + 1)][:, None]


def spread_kernel(sections, place, shifted_ref, loss_ref, blocks_ref, rows_ref):
    last = (lax.axis_index("section") == sections - 1).astype(jnp.int32)
    chosen = jnp.where(jnp.full(rows_ref.shape, last) > 0, loss_ref[place], shifted_ref[...])
    rows_ref[...] = chosen
    blocks_ref[...] = jnp.broadcast_to(chosen[None], blocks_ref.shape)


def forward_kernel(x_ref, weights_ref, *refs):
    slope_ref, hidden_ref = refs[-2:]
    x = x_ref[...]
    for cols in parts(weights_ref.shape[1]):
        relu = jnp.maximum(mm(x, weights_ref[:, cols]), 0.0)
        slope_ref[:, cols] = 2.0 * relu
        hidden_ref[:, cols] = (relu * relu).astype(BF16)


def masked_sums(slot, lengths_ref, paired):
    cut = lengths_ref[0:1, slot : slot + 1]
    tokens = paired.shape[0]
    row = lax.broadcasted_iota(jnp.int32, (tokens, tokens), 0) < cut
    col = lax.broadcasted_iota(jnp.int32, (tokens, tokens), 1) < cut
    before = jnp.sum(jnp.where(row & col, paired, 0.0), axis=(0, 1), keepdims=True)
    after = jnp.sum(jnp.where(row | col, 0.0, paired), axis=(0, 1), keepdims=True)
    lane = lax.broadcasted_iota(jnp.int32, (1, LANES), 1)
    return jnp.where(lane == 2 * slot, before, jnp.where(lane == 2 * slot + 1, after, 0.0))


def back_products(grads, slope_ref, w_out_ref, w_in_ref, dz_ref, share_ref):
    for part in parts(w_out_ref.shape[0]):
        back = nt(grads, w_out_ref[part, :])
        dz_ref[:, part] = (slope_ref[:, part] * back).astype(BF16)
    dz = dz_ref[...]
    for part in parts(w_in_ref.shape[0]):
        share_ref[:, part] = nt(dz, w_in_ref[part, :]).astype(BF16)
    return dz


def back_kernel(grads_ref, slope_ref, w_out_ref, w_in_ref, dz_ref, share_ref):
    back_products(grads_ref[...], slope_ref, w_out_ref, w_in_ref, dz_ref, share_ref)


def last_back_kernel(
    slot, lengths_ref, grads_ref, slope_ref, w_out_ref, w_in_ref, gram_x_ref, gram_h_ref, *refs
):
    *sums_refs, dz_ref, share_ref = refs
    grads = grads_ref[...]
    dz = back_products(grads, slope_ref, w_out_ref, w_in_ref, dz_ref, share_ref)
    paired = gram_x_ref[...] * nt(dz, dz) + gram_h_ref[...] * nt(grads, grads)
    total = masked_sums(slot, lengths_ref, paired)
    for sums_ref in sums_refs:
        total = total + sums_ref[...]
    high = total.astype(BF16)
    rest = total - high.astype(F32)
    middle = rest.astype(BF16)
    low = (rest - middle.astype(F32)).astype(BF16)
    line = high.astype(F32)
    for place, piece in ((1, middle), (2, low)):
        line = line + pltpu.roll(piece.astype(F32), place * SPACING, 1)
    share_ref[:, D:] = jnp.broadcast_to(line, (share_ref.shape[0], LANES)).astype(BF16)


def squares_kernel(slot, lengths_ref, x_ref, hidden_ref, grads_ref, dz_ref, sums_ref):
    x, hidden, grads, dz = x_ref[...], hidden_ref[...], grads_ref[...], dz_ref[...]
    paired = nt(x, x) * nt(dz, dz) + nt(hidden, hidden) * nt(grads, grads)
    sums_ref[...] = masked_sums(slot, lengths_ref, paired)


def grams_kernel(x_ref, hidden_ref, gram_x_ref, gram_h_ref):
    x, hidden = x_ref[...], hidden_ref[...]
    gram_x_ref[...] = nt(x, x)
    gram_h_ref[...] = nt(hidden, hidden)


def sum_kernel(arrived_ref, incoming_ref, passing_ref):
    total = incoming_ref[...].astype(F32)
    for peer in range(arrived_ref.shape[0]):
        total = total + arrived_ref[peer].astype(F32)
    passing_ref[...] = total.astype(BF16)


def last_sum_kernel(arrived_ref, incoming_ref, *refs):
    *earlier_refs, results_ref, line_ref = refs
    total = incoming_ref[...].astype(F32)
    line = jnp.zeros(line_ref.shape, F32)
    for peer in range(arrived_ref.shape[0]):
        total = total + arrived_ref[peer, :, :D].astype(F32)
        line = line + arrived_ref[peer, 0:1, D:].astype(F32)
    for place, earlier_ref in enumerate(earlier_refs):
        results_ref[place] = earlier_ref[...]
    results_ref[len(earlier_refs)] = total.astype(BF16)
    pieces = [pltpu.roll(line, LANES - place * SPACING, 1) for place in (1, 2)]
    line_ref[...] = line + (pieces[0] + pieces[1])


def final_kernel(slots, lengths_ref, totals_ref, *refs):
    x, hidden, dz, dy = (refs[i * slots : (i + 1) * slots] for i in range(4))
    grad_in_ref, grad_out_ref, dzc_ref, dyc_ref = refs[4 * slots :]
    tokens = dz[0].shape[0]
    step = pl.program_id(0)

    @pl.when(step == 0)
    def _():
        factor = 1.0 / (jnp.sqrt(totals_ref[...] / (D * FF)) + GAMMA)
        for slot in range(slots):
            cut = lengths_ref[0:1, slot : slot + 1]
            row = lax.broadcasted_iota(jnp.int32, (tokens, 1), 0) < cut
            scale = jnp.where(
                row,
                factor[:, 2 * slot : 2 * slot + 1],
                factor[:, 2 * slot + 1 : 2 * slot + 2],
            )
            rows = slice(slot * tokens, (slot + 1) * tokens)
            dzc_ref[rows, :] = (dz[slot][...].astype(F32) * scale).astype(BF16)
            dyc_ref[rows, :] = (dy[slot][...].astype(F32) * scale).astype(BF16)

    block = grad_in_ref.shape[0]
    strip = pl.ds(pl.multiple_of(step * block, block), block)
    for left, right_ref, out_ref in ((x, dzc_ref, grad_in_ref), (hidden, dyc_ref, grad_out_ref)):
        for cols in parts(right_ref.shape[1]):
            total = tn(left[0][:, strip], right_ref[:tokens, cols])
            for slot in range(1, slots):
                rows = slice(slot * tokens, (slot + 1) * tokens)
                total = total + tn(left[slot][:, strip], right_ref[rows, cols])
            out_ref[:, cols] = total.astype(BF16)


def final_products(lengths, totals, x, hidden, dz, dy):
    slots = len(dz)
    tokens, width = dz[0].shape
    rows = x[0].shape[1]
    block = 256
    out = pl.BlockSpec((block, width), lambda i: (i, 0))
    return pl.pallas_call(
        lambda *refs: final_kernel(slots, *refs),
        grid=(rows // block,),
        out_shape=(shape(rows, width), shape(rows, width)),
        in_specs=[VMEM] * (2 + 4 * slots),
        out_specs=(out, out),
        scratch_shapes=[pltpu.VMEM((slots * tokens, width), BF16)] * 2,
        name="final",
        compiler_params=pltpu.CompilerParams(vmem_limit_bytes=12 * MIB),
        cost_estimate=pl.CostEstimate(
            flops=4 * rows * width * slots * tokens, bytes_accessed=4 * MIB, transcendentals=0
        ),
    )(lengths, totals, *x, *hidden, *dz, *dy)


def exchange(blocks):
    return lax.all_to_all(blocks, "tensor", split_axis=0, concat_axis=0, tiled=True)


def gather_along_x(block):
    count = lax.axis_size("tensor")
    blocks = [block]
    for distance in range(1, ALONG_X):
        pairs = [
            (at, at // ALONG_X * ALONG_X + (at + distance) % ALONG_X) for at in range(count)
        ]
        blocks.append(lax.ppermute(block, "tensor", pairs))
    along_z, rows, width = block.shape
    outs = (shape(along_z, ALONG_X, rows, D),) * (width // D)
    gathered = call(assemble_kernel, outs, blocks, 0, "assemble")
    return [out.reshape(count * rows, D) for out in gathered]


def per_device(saved_inputs, slot_index, example_lengths, first_grads, loss_grads, w_in, w_out):
    sections, count = lax.axis_size("section"), lax.axis_size("tensor")
    first, second = w_in[0], w_out[0]
    slots = loss_grads.shape[0] + 1
    rows = first_grads.shape[1]
    tokens = count * rows
    units = first.shape[1]
    lengths = example_lengths[0].T
    incoming = first_grads[0]
    product = 2 * tokens * D * units
    square = (tokens, tokens)

    along_z = count // ALONG_X
    blocks = pl.pallas_call(
        start_kernel,
        out_shape=shape(along_z, rows, (slots + 1) * D),
        in_specs=[pl.BlockSpec(memory_space=pl.ANY)] * 3,
        out_specs=VMEM,
        scratch_shapes=[
            pltpu.VMEM(slot_index.shape, jnp.int32),
            pltpu.VMEM(saved_inputs.shape[1:], BF16),
            pltpu.VMEM((rows, D), BF16),
            pltpu.SemaphoreType.DMA((3,)),
        ],
        name="start",
        compiler_params=pltpu.CompilerParams(vmem_limit_bytes=60 * MIB),
    )(slot_index, saved_inputs[0], incoming)
    groups = [[z * ALONG_X + x for z in range(along_z)] for x in range(ALONG_X)]
    begun = lax.all_to_all(
        blocks, "tensor", split_axis=0, concat_axis=0, axis_index_groups=groups, tiled=True
    )
    halves = (shape(along_z, rows, 2 * D), shape(along_z, rows, (slots - 1) * D))
    urgent, later = call(split_kernel, halves, (begun,), 0, "split")
    x, grads = gather_along_x(urgent)
    later = gather_along_x(later)

    def forward(x, *early):
        outs = (shape(tokens, units, dtype=F32), shape(tokens, units))
        return call(forward_kernel, outs, (x, first, *early), product, "forward")

    slope, hidden = forward(x, second)
    xs, hiddens, dzs, dys, results, squares = [], [], [], [], [], []
    for slot in range(slots):
        xs.append(x)
        hiddens.append(hidden)
        dys.append(grads)
        if slot + 1 == slots:
            break
        dz, share = call(
            back_kernel,
            (shape(tokens, units), shape(tokens, D)),
            (grads, slope, second, first),
            2 * product,
            "back",
        )
        dzs.append(dz)
        arrived = exchange(share.reshape(count, rows, D))
        passing = call(sum_kernel, shape(rows, D), (arrived, incoming), tokens * D, "add_up")
        results.append(passing)
        shifted = lax.ppermute(
            passing, "section", [(source, source - 1) for source in range(1, sections)]
        )
        held = lax.optimization_barrier((passing, x, hidden, grads, dz, later[slot]))
        one = call(
            lambda *refs, slot=slot: squares_kernel(slot, *refs),
            shape(1, LANES, dtype=F32),
            (lengths, *held[1:5]),
            product,
            "squares",
        )
        squares.append(one)
        x = held[5]
        slope, hidden = forward(x)
        ready = [one, slope, hidden]
        if slot + 2 == slots:
            ready += call(
                grams_kernel, (shape(*square, dtype=F32),) * 2, (x, hidden), product // 4, "grams"
            )
        shifted, squares[-1], slope, hidden, *grams = lax.optimization_barrier((shifted, *ready))
        blocks, incoming = call(
            lambda *refs, slot=slot: spread_kernel(sections, slot, *refs),
            (shape(count, rows, D), shape(rows, D)),
            (shifted, loss_grads),
            0,
            "spread",
        )
        grads = exchange(blocks).reshape(tokens, D)

    dz, share = call(
        lambda *refs: last_back_kernel(slots - 1, *refs),
        (shape(tokens, units), shape(tokens, D + LANES)),
        (lengths, grads, slope, second, first, *grams, *squares),
        2 * product,
        "last_back",
    )
    dzs.append(dz)
    arrived = exchange(share.reshape(count, rows, D + LANES))
    results, totals = call(
        last_sum_kernel,
        (shape(slots, rows, D), shape(1, LANES, dtype=F32)),
        (arrived, incoming, *results),
        tokens * D,
        "last_add_up",
    )
    grad_in, grad_out = final_products(lengths, totals, xs, hiddens, dzs, dys)
    return grad_in[None], grad_out[None], results[None]


def solution(mesh):
    return jax.shard_map(
        per_device,
        mesh=mesh,
        in_specs=(
            P("section", None, "tensor", None),
            P("section", None),
            P("section", None, None),
            P("section", "tensor", None),
            P(None, "tensor", None),
            P("section", None, "tensor"),
            P("section", "tensor", None),
        ),
        out_specs=(
            P("section", None, "tensor"),
            P("section", "tensor", None),
            P("section", None, "tensor", None),
        ),
        check_vma=False,
    )
```

```python
import jax
import jax.numpy as jnp
from jax import lax
from jax.experimental import pallas as pl
from jax.experimental.pallas import tpu as pltpu
from jax.sharding import PartitionSpec as P

D = 1024
FF = 32768
GAMMA = 0.01
F32 = jnp.float32
BF16 = jnp.bfloat16
MIB = 1 << 20
STEP = 256
LANES = 128
SPACING = 32
ALONG_X = 4

VMEM = pl.BlockSpec(memory_space=pltpu.VMEM)


def shape(*dims, dtype=BF16):
    return jax.ShapeDtypeStruct(dims, dtype)


def call(kernel, outs, operands, flops, name):
    return pl.pallas_call(
        kernel,
        out_shape=outs,
        in_specs=[VMEM] * len(operands),
        out_specs=jax.tree.map(lambda _: VMEM, outs),
        name=name,
        compiler_params=pltpu.CompilerParams(vmem_limit_bytes=8 * MIB),
        cost_estimate=pl.CostEstimate(flops=flops, bytes_accessed=MIB, transcendentals=0),
    )(*operands)


def parts(extent):
    return [slice(at, at + STEP) for at in range(0, extent, STEP)]


def nt(a, b):
    return lax.dot_general(a, b, (((1,), (1,)), ((), ())), preferred_element_type=F32)


def tn(a, b):
    return lax.dot_general(a, b, (((0,), (0,)), ((), ())), preferred_element_type=F32)


def mm(a, b):
    return jnp.dot(a, b, preferred_element_type=F32)


def start_kernel(index, saved, grads, blocks_ref, index_v, saved_v, grads_v, sems):
    loads = [
        pltpu.make_async_copy(source, target, sems.at[place])
        for place, (source, target) in enumerate(
            ((index, index_v), (saved, saved_v), (grads, grads_v))
        )
    ]
    for load in loads:
        load.start()
    for load in loads:
        load.wait()
    count, rows, width = blocks_ref.shape
    for slot in range(index_v.shape[1]):
        wanted = index_v[:, slot : slot + 1]
        x = saved_v[0]
        for place in range(1, saved_v.shape[0]):
            x = jnp.where(wanted == place, saved_v[place], x)
        at = slot + 1 if slot else 0
        blocks_ref[:, :, D * at : D * (at + 1)] = jnp.broadcast_to(x[None], (count, rows, D))
    blocks_ref[:, :, D : 2 * D] = jnp.broadcast_to(grads_v[...][None], (count, rows, D))


def split_kernel(begun_ref, loss_ref, urgent_ref, later_ref):
    along_z, _, width = urgent_ref.shape
    urgent_ref[...] = begun_ref[:, :, :width]
    later_ref[:along_z] = begun_ref[:, :, width:]
    for place in range(loss_ref.shape[0]):
        later_ref[along_z, :, D * place : D * (place + 1)] = loss_ref[place]


def assemble_kernel(*refs):
    blocks, out_refs = refs[:ALONG_X], refs[ALONG_X:]
    mine = lax.axis_index("tensor") % ALONG_X
    for distance, block_ref in enumerate(blocks):
        source = (mine + (ALONG_X - distance)) % ALONG_X
        done = {}
        for out_ref in out_refs:
            deep = out_ref.shape[0]
            top = 0 if deep == out_refs[0].shape[0] else out_refs[0].shape[0]
            at = done.get(top, 0)
            done[top] = at + D
            out_ref[:, pl.ds(source, 1)] = block_ref[top : top + deep, :, at : at + D][:, None]


def partial_kernel(arrived_ref, grads_ref, partial_ref, both_ref):
    total = arrived_ref[0].astype(F32)
    for peer in range(1, arrived_ref.shape[0]):
        total = total + arrived_ref[peer].astype(F32)
    total = total.astype(BF16)
    partial_ref[...] = total
    both_ref[:, :D] = total
    both_ref[:, D:] = grads_ref[lax.axis_index("tensor") // ALONG_X]


def combine_kernel(sections, both_ref, *refs):
    *parts_refs, loss_ref, blocks_ref, own_ref = refs
    first, second, third = [ref[...].astype(F32) for ref in parts_refs]
    total = (both_ref[:, :D].astype(F32) + second) + (first + third)
    passing = (both_ref[:, D:].astype(F32) + total).astype(BF16)
    rows = own_ref.shape[0]
    mine = lax.axis_index("tensor") % ALONG_X
    for x in range(ALONG_X):

        @pl.when(mine == x)
        def _():
            own_ref[...] = passing[rows * x : rows * (x + 1)]

    last = (lax.axis_index("section") == sections - 1).astype(jnp.int32)
    loss = loss_ref[0].reshape(passing.shape)
    chosen = jnp.where(jnp.full(passing.shape, last) > 0, loss, passing)
    blocks_ref[...] = jnp.broadcast_to(chosen[None], blocks_ref.shape)


def forward_kernel(x_ref, weights_ref, *refs):
    slope_ref, hidden_ref = refs[-2:]
    x = x_ref[...]
    for cols in parts(weights_ref.shape[1]):
        relu = jnp.maximum(mm(x, weights_ref[:, cols]), 0.0)
        slope_ref[:, cols] = 2.0 * relu
        hidden_ref[:, cols] = (relu * relu).astype(BF16)


def masked_sums(slot, lengths_ref, paired):
    cut = lengths_ref[0:1, slot : slot + 1]
    tokens = paired.shape[0]
    row = lax.broadcasted_iota(jnp.int32, (tokens, tokens), 0) < cut
    col = lax.broadcasted_iota(jnp.int32, (tokens, tokens), 1) < cut
    before = jnp.sum(jnp.where(row & col, paired, 0.0), axis=(0, 1), keepdims=True)
    after = jnp.sum(jnp.where(row | col, 0.0, paired), axis=(0, 1), keepdims=True)
    lane = lax.broadcasted_iota(jnp.int32, (1, LANES), 1)
    return jnp.where(lane == 2 * slot, before, jnp.where(lane == 2 * slot + 1, after, 0.0))


def back_products(grads, slope_ref, w_out_ref, w_in_ref, dz_ref, share_ref):
    for part in parts(w_out_ref.shape[0]):
        back = nt(grads, w_out_ref[part, :])
        dz_ref[:, part] = (slope_ref[:, part] * back).astype(BF16)
    dz = dz_ref[...]
    for part in parts(w_in_ref.shape[0]):
        share_ref[:, part] = nt(dz, w_in_ref[part, :]).astype(BF16)
    return dz


def back_kernel(grads_ref, slope_ref, w_out_ref, w_in_ref, dz_ref, share_ref):
    back_products(grads_ref[...], slope_ref, w_out_ref, w_in_ref, dz_ref, share_ref)


def last_back_kernel(
    slot, lengths_ref, grads_ref, slope_ref, w_out_ref, w_in_ref, gram_x_ref, gram_h_ref, *refs
):
    *sums_refs, dz_ref, share_ref = refs
    grads = grads_ref[...]
    dz = back_products(grads, slope_ref, w_out_ref, w_in_ref, dz_ref, share_ref)
    paired = gram_x_ref[...] * nt(dz, dz) + gram_h_ref[...] * nt(grads, grads)
    total = masked_sums(slot, lengths_ref, paired)
    for sums_ref in sums_refs:
        total = total + sums_ref[...]
    high = total.astype(BF16)
    rest = total - high.astype(F32)
    middle = rest.astype(BF16)
    low = (rest - middle.astype(F32)).astype(BF16)
    line = high.astype(F32)
    for place, piece in ((1, middle), (2, low)):
        line = line + pltpu.roll(piece.astype(F32), place * SPACING, 1)
    share_ref[:, D:] = jnp.broadcast_to(line, (share_ref.shape[0], LANES)).astype(BF16)


def squares_kernel(slot, lengths_ref, x_ref, hidden_ref, grads_ref, dz_ref, sums_ref):
    x, hidden, grads, dz = x_ref[...], hidden_ref[...], grads_ref[...], dz_ref[...]
    paired = nt(x, x) * nt(dz, dz) + nt(hidden, hidden) * nt(grads, grads)
    sums_ref[...] = masked_sums(slot, lengths_ref, paired)


def grams_kernel(x_ref, hidden_ref, gram_x_ref, gram_h_ref):
    x, hidden = x_ref[...], hidden_ref[...]
    gram_x_ref[...] = nt(x, x)
    gram_h_ref[...] = nt(hidden, hidden)


def last_sum_kernel(arrived_ref, grads_ref, *refs):
    *earlier_refs, results_ref, line_ref = refs
    total = grads_ref[lax.axis_index("tensor")].astype(F32)
    line = jnp.zeros(line_ref.shape, F32)
    for peer in range(arrived_ref.shape[0]):
        total = total + arrived_ref[peer, :, :D].astype(F32)
        line = line + arrived_ref[peer, 0:1, D:].astype(F32)
    for place, earlier_ref in enumerate(earlier_refs):
        results_ref[place] = earlier_ref[...]
    results_ref[len(earlier_refs)] = total.astype(BF16)
    pieces = [pltpu.roll(line, LANES - place * SPACING, 1) for place in (1, 2)]
    line_ref[...] = line + (pieces[0] + pieces[1])


def final_kernel(slots, lengths_ref, totals_ref, *refs):
    x, hidden, dz, dy = (refs[i * slots : (i + 1) * slots] for i in range(4))
    grad_in_ref, grad_out_ref, dzc_ref, dyc_ref = refs[4 * slots :]
    tokens = dz[0].shape[0]
    step = pl.program_id(0)

    @pl.when(step == 0)
    def _():
        factor = 1.0 / (jnp.sqrt(totals_ref[...] / (D * FF)) + GAMMA)
        for slot in range(slots):
            cut = lengths_ref[0:1, slot : slot + 1]
            row = lax.broadcasted_iota(jnp.int32, (tokens, 1), 0) < cut
            scale = jnp.where(
                row,
                factor[:, 2 * slot : 2 * slot + 1],
                factor[:, 2 * slot + 1 : 2 * slot + 2],
            )
            rows = slice(slot * tokens, (slot + 1) * tokens)
            dzc_ref[rows, :] = (dz[slot][...].astype(F32) * scale).astype(BF16)
            dyc_ref[rows, :] = (dy[slot][...].astype(F32) * scale).astype(BF16)

    block = grad_in_ref.shape[0]
    strip = pl.ds(pl.multiple_of(step * block, block), block)
    for left, right_ref, out_ref in ((x, dzc_ref, grad_in_ref), (hidden, dyc_ref, grad_out_ref)):
        for cols in parts(right_ref.shape[1]):
            total = tn(left[0][:, strip], right_ref[:tokens, cols])
            for slot in range(1, slots):
                rows = slice(slot * tokens, (slot + 1) * tokens)
                total = total + tn(left[slot][:, strip], right_ref[rows, cols])
            out_ref[:, cols] = total.astype(BF16)


def final_products(lengths, totals, x, hidden, dz, dy):
    slots = len(dz)
    tokens, width = dz[0].shape
    rows = x[0].shape[1]
    block = 256
    out = pl.BlockSpec((block, width), lambda i: (i, 0))
    return pl.pallas_call(
        lambda *refs: final_kernel(slots, *refs),
        grid=(rows // block,),
        out_shape=(shape(rows, width), shape(rows, width)),
        in_specs=[VMEM] * (2 + 4 * slots),
        out_specs=(out, out),
        scratch_shapes=[pltpu.VMEM((slots * tokens, width), BF16)] * 2,
        name="final",
        compiler_params=pltpu.CompilerParams(vmem_limit_bytes=12 * MIB),
        cost_estimate=pl.CostEstimate(
            flops=4 * rows * width * slots * tokens, bytes_accessed=4 * MIB, transcendentals=0
        ),
    )(lengths, totals, *x, *hidden, *dz, *dy)


def exchange(blocks):
    return lax.all_to_all(blocks, "tensor", split_axis=0, concat_axis=0, tiled=True)


def exchange_along_z(blocks):
    count = lax.axis_size("tensor")
    groups = [list(range(x, count, ALONG_X)) for x in range(ALONG_X)]
    return lax.all_to_all(
        blocks, "tensor", split_axis=0, concat_axis=0, axis_index_groups=groups, tiled=True
    )


def moved(value, sections_back, distance):
    sections, count = lax.axis_size("section"), lax.axis_size("tensor")
    pairs = [
        (
            section * count + at,
            (section - sections_back) % sections * count
            + at // ALONG_X * ALONG_X
            + (at + distance) % ALONG_X,
        )
        for section in range(sections)
        for at in range(count)
    ]
    return lax.ppermute(value, ("section", "tensor"), pairs)


def gather_along_x(block, along_z):
    blocks = [block] + [moved(block, 0, distance) for distance in range(1, ALONG_X)]
    deep, rows, width = block.shape
    outs = [shape(along_z, ALONG_X, rows, D)] * (width // D)
    if deep > along_z:
        outs += [shape(deep - along_z, ALONG_X, rows, D)] * (width // D)
    return call(assemble_kernel, outs, blocks, 0, "assemble")


def per_device(saved_inputs, slot_index, example_lengths, first_grads, loss_grads, w_in, w_out):
    sections, count = lax.axis_size("section"), lax.axis_size("tensor")
    first, second = w_in[0], w_out[0]
    slots = loss_grads.shape[0] + 1
    rows = first_grads.shape[1]
    tokens = count * rows
    units = first.shape[1]
    lengths = example_lengths[0].T
    incoming = first_grads[0]
    product = 2 * tokens * D * units
    square = (tokens, tokens)

    along_z = count // ALONG_X
    blocks = pl.pallas_call(
        start_kernel,
        out_shape=shape(along_z, rows, (slots + 1) * D),
        in_specs=[pl.BlockSpec(memory_space=pl.ANY)] * 3,
        out_specs=VMEM,
        scratch_shapes=[
            pltpu.VMEM(slot_index.shape, jnp.int32),
            pltpu.VMEM(saved_inputs.shape[1:], BF16),
            pltpu.VMEM((rows, D), BF16),
            pltpu.SemaphoreType.DMA((3,)),
        ],
        name="start",
        compiler_params=pltpu.CompilerParams(vmem_limit_bytes=60 * MIB),
    )(slot_index, saved_inputs[0], incoming)
    begun = exchange_along_z(blocks)
    halves = (shape(along_z, rows, 2 * D), shape(along_z + 1, rows, (slots - 1) * D))
    urgent, later = call(split_kernel, halves, (begun, loss_grads), 0, "split")
    x, grads = [part.reshape(tokens, D) for part in gather_along_x(urgent, along_z)]

    def forward(x, *early):
        outs = (shape(tokens, units, dtype=F32), shape(tokens, units))
        return call(forward_kernel, outs, (x, first, *early), product, "forward")

    slope, hidden = forward(x, second)
    xs, hiddens, dzs, dys, results, squares = [], [], [], [], [], []
    for slot in range(slots):
        xs.append(x)
        hiddens.append(hidden)
        dys.append(grads)
        if slot + 1 == slots:
            break
        dz, share = call(
            back_kernel,
            (shape(tokens, units), shape(tokens, D)),
            (grads, slope, second, first),
            2 * product,
            "back",
        )
        dzs.append(dz)
        by_z = (along_z, tokens // along_z, D)
        arrived = exchange_along_z(share.reshape(by_z))
        partial, both = call(
            partial_kernel,
            (shape(*by_z[1:]), shape(by_z[1], 2 * D)),
            (arrived, grads.reshape(by_z)),
            tokens * D,
            "partial",
        )
        if slot:
            partial, both, results[-1] = lax.optimization_barrier((partial, both, results[-1]))
            results[-1] = moved(results[-1], -1, 0)
        else:
            partial, both, later = lax.optimization_barrier((partial, both, later))
        pieces = [moved(both, 1, 0)]
        pieces += [moved(partial, 1, distance) for distance in range(1, ALONG_X)]
        if not slot:
            later = gather_along_x(later, along_z)
            later, loss = later[: slots - 1], later[slots - 1 :]
        held = lax.optimization_barrier((partial, x, hidden, grads, dz, later[slot]))
        one = call(
            lambda *refs, slot=slot: squares_kernel(slot, *refs),
            shape(1, LANES, dtype=F32),
            (lengths, *held[1:5]),
            product,
            "squares",
        )
        squares.append(one)
        x = held[5].reshape(tokens, D)
        slope, hidden = forward(x)
        ready = [one, slope, hidden, results[-1] if slot else later[1]]
        if slot + 2 == slots:
            ready += call(
                grams_kernel, (shape(*square, dtype=F32),) * 2, (x, hidden), product // 4, "grams"
            )
        pieces[0], squares[-1], slope, hidden, other, *grams = lax.optimization_barrier(
            (pieces[0], *ready)
        )
        if slot:
            results[-1] = other
        blocks, own = call(
            lambda *refs: combine_kernel(sections, *refs),
            (shape(*by_z), shape(rows, D)),
            (*pieces, loss[slot]),
            0,
            "combine",
        )
        results.append(own)
        grads = exchange_along_z(blocks).reshape(tokens, D)

    grads, results[-1] = lax.optimization_barrier((grads, results[-1]))
    results[-1] = moved(results[-1], -1, 0)
    dz, share = call(
        lambda *refs: last_back_kernel(slots - 1, *refs),
        (shape(tokens, units), shape(tokens, D + LANES)),
        (lengths, grads, slope, second, first, *grams, *squares),
        2 * product,
        "last_back",
    )
    dzs.append(dz)
    share, results[-1] = lax.optimization_barrier((share, results[-1]))
    arrived = exchange(share.reshape(count, rows, D + LANES))
    results, totals = call(
        last_sum_kernel,
        (shape(slots, rows, D), shape(1, LANES, dtype=F32)),
        (arrived, grads.reshape(count, rows, D), *results),
        tokens * D,
        "last_add_up",
    )
    grad_in, grad_out = final_products(lengths, totals, xs, hiddens, dzs, dys)
    return grad_in[None], grad_out[None], results[None]


def solution(mesh):
    return jax.shard_map(
        per_device,
        mesh=mesh,
        in_specs=(
            P("section", None, "tensor", None),
            P("section", None),
            P("section", None, None),
            P("section", "tensor", None),
            P(None, "tensor", None),
            P("section", None, "tensor"),
            P("section", "tensor", None),
        ),
        out_specs=(
            P("section", None, "tensor"),
            P("section", "tensor", None),
            P("section", None, "tensor", None),
        ),
        check_vma=False,
    )
```

```python
import jax
import jax.numpy as jnp
from jax import lax
from jax.experimental import pallas as pl
from jax.experimental.pallas import tpu as pltpu
from jax.sharding import PartitionSpec as P

D = 1024
FF = 32768
GAMMA = 0.01
F32 = jnp.float32
BF16 = jnp.bfloat16
MIB = 1 << 20
STEP = 256
LANES = 128
SPACING = 32
ALONG_X = 4

VMEM = pl.BlockSpec(memory_space=pltpu.VMEM)


def shape(*dims, dtype=BF16):
    return jax.ShapeDtypeStruct(dims, dtype)


def call(kernel, outs, operands, flops, name):
    return pl.pallas_call(
        kernel,
        out_shape=outs,
        in_specs=[VMEM] * len(operands),
        out_specs=jax.tree.map(lambda _: VMEM, outs),
        name=name,
        compiler_params=pltpu.CompilerParams(vmem_limit_bytes=8 * MIB),
        cost_estimate=pl.CostEstimate(flops=flops, bytes_accessed=MIB, transcendentals=0),
    )(*operands)


def parts(extent):
    return [slice(at, at + STEP) for at in range(0, extent, STEP)]


def nt(a, b):
    return lax.dot_general(a, b, (((1,), (1,)), ((), ())), preferred_element_type=F32)


def tn(a, b):
    return lax.dot_general(a, b, (((0,), (0,)), ((), ())), preferred_element_type=F32)


def mm(a, b):
    return jnp.dot(a, b, preferred_element_type=F32)


def start_kernel(index, saved, grads, blocks_ref, index_v, saved_v, grads_v, sems):
    loads = [
        pltpu.make_async_copy(source, target, sems.at[place])
        for place, (source, target) in enumerate(
            ((index, index_v), (saved, saved_v), (grads, grads_v))
        )
    ]
    for load in loads:
        load.start()
    for load in loads:
        load.wait()
    count, rows, width = blocks_ref.shape
    for slot in range(index_v.shape[1]):
        wanted = index_v[:, slot : slot + 1]
        x = saved_v[0]
        for place in range(1, saved_v.shape[0]):
            x = jnp.where(wanted == place, saved_v[place], x)
        at = slot + 1 if slot else 0
        blocks_ref[:, :, D * at : D * (at + 1)] = jnp.broadcast_to(x[None], (count, rows, D))
    blocks_ref[:, :, D : 2 * D] = jnp.broadcast_to(grads_v[...][None], (count, rows, D))


def split_kernel(begun_ref, *out_refs):
    width = out_refs[0].shape[-1]
    for place, out_ref in enumerate(out_refs):
        out_ref[...] = begun_ref[:, :, width * place : width * (place + 1)]


def assemble_kernel(*refs):
    blocks, out_refs = refs[:ALONG_X], refs[ALONG_X:]
    mine = lax.axis_index("tensor") % ALONG_X
    for distance, block_ref in enumerate(blocks):
        source = (mine + (ALONG_X - distance)) % ALONG_X
        for place, out_ref in enumerate(out_refs):
            out_ref[:, pl.ds(source, 1)] = block_ref[:, :, D * place : D * (place + 1)][:, None]


def forward_kernel(x_ref, weights_ref, slope_ref, hidden_ref):
    x = x_ref[...]
    for cols in parts(weights_ref.shape[1]):
        relu = jnp.maximum(mm(x, weights_ref[:, cols]), 0.0)
        slope_ref[:, cols] = 2.0 * relu
        hidden_ref[:, cols] = (relu * relu).astype(BF16)


def masked_sums(slot, lengths_ref, paired):
    cut = lengths_ref[0:1, slot : slot + 1]
    tokens = paired.shape[0]
    row = lax.broadcasted_iota(jnp.int32, (tokens, tokens), 0) < cut
    col = lax.broadcasted_iota(jnp.int32, (tokens, tokens), 1) < cut
    before = jnp.sum(jnp.where(row & col, paired, 0.0), axis=(0, 1), keepdims=True)
    after = jnp.sum(jnp.where(row | col, 0.0, paired), axis=(0, 1), keepdims=True)
    lane = lax.broadcasted_iota(jnp.int32, (1, LANES), 1)
    return jnp.where(lane == 2 * slot, before, jnp.where(lane == 2 * slot + 1, after, 0.0))


def back_products(grads, slope_ref, w_out_ref, w_in_ref, dz_ref, share_ref):
    for part in parts(w_out_ref.shape[0]):
        back = nt(grads, w_out_ref[part, :])
        dz_ref[:, part] = (slope_ref[:, part] * back).astype(BF16)
    dz = dz_ref[...]
    for part in parts(w_in_ref.shape[0]):
        share_ref[:, part] = nt(dz, w_in_ref[part, :]).astype(BF16)
    return dz


def back_kernel(grads_ref, slope_ref, w_out_ref, w_in_ref, dz_ref, share_ref):
    back_products(grads_ref[...], slope_ref, w_out_ref, w_in_ref, dz_ref, share_ref)


def last_back_kernel(
    slot, lengths_ref, grads_ref, slope_ref, w_out_ref, w_in_ref, gram_x_ref, gram_h_ref, *refs
):
    *sums_refs, dz_ref, share_ref = refs
    grads = grads_ref[...]
    dz = back_products(grads, slope_ref, w_out_ref, w_in_ref, dz_ref, share_ref)
    paired = gram_x_ref[...] * nt(dz, dz) + gram_h_ref[...] * nt(grads, grads)
    total = masked_sums(slot, lengths_ref, paired)
    for sums_ref in sums_refs:
        total = total + sums_ref[...]
    high = total.astype(BF16)
    rest = total - high.astype(F32)
    middle = rest.astype(BF16)
    low = (rest - middle.astype(F32)).astype(BF16)
    line = high.astype(F32)
    for place, piece in ((1, middle), (2, low)):
        line = line + pltpu.roll(piece.astype(F32), place * SPACING, 1)
    share_ref[:, D:] = jnp.broadcast_to(line, (share_ref.shape[0], LANES)).astype(BF16)


def squares_kernel(slot, lengths_ref, x_ref, hidden_ref, grads_ref, dz_ref, sums_ref):
    x, hidden, grads, dz = x_ref[...], hidden_ref[...], grads_ref[...], dz_ref[...]
    paired = nt(x, x) * nt(dz, dz) + nt(hidden, hidden) * nt(grads, grads)
    sums_ref[...] = masked_sums(slot, lengths_ref, paired)


def grams_kernel(x_ref, hidden_ref, gram_x_ref, gram_h_ref):
    x, hidden = x_ref[...], hidden_ref[...]
    gram_x_ref[...] = nt(x, x)
    gram_h_ref[...] = nt(hidden, hidden)


def sum_kernel(place, arrived_ref, grads_ref, loss_ref, passing_ref, blocks_ref):
    total = grads_ref[lax.axis_index("tensor")].astype(F32)
    for peer in range(arrived_ref.shape[0]):
        total = total + arrived_ref[peer].astype(F32)
    passing = total.astype(BF16)
    passing_ref[...] = passing
    first = (lax.axis_index("section") == 0).astype(jnp.int32)
    chosen = jnp.where(jnp.full(passing.shape, first) > 0, loss_ref[place], passing)
    blocks_ref[...] = jnp.broadcast_to(chosen[None], blocks_ref.shape)


def last_sum_kernel(arrived_ref, grads_ref, *refs):
    *earlier_refs, results_ref, line_ref = refs
    total = grads_ref[lax.axis_index("tensor")].astype(F32)
    line = jnp.zeros(line_ref.shape, F32)
    for peer in range(arrived_ref.shape[0]):
        total = total + arrived_ref[peer, :, :D].astype(F32)
        line = line + arrived_ref[peer, 0:1, D:].astype(F32)
    for place, earlier_ref in enumerate(earlier_refs):
        results_ref[place] = earlier_ref[...]
    results_ref[len(earlier_refs)] = total.astype(BF16)
    pieces = [pltpu.roll(line, LANES - place * SPACING, 1) for place in (1, 2)]
    line_ref[...] = line + (pieces[0] + pieces[1])


def final_kernel(slots, lengths_ref, totals_ref, *refs):
    x, hidden, dz, dy = (refs[i * slots : (i + 1) * slots] for i in range(4))
    grad_in_ref, grad_out_ref, dzc_ref, dyc_ref = refs[4 * slots :]
    tokens = dz[0].shape[0]
    step = pl.program_id(0)

    @pl.when(step == 0)
    def _():
        factor = 1.0 / (jnp.sqrt(totals_ref[...] / (D * FF)) + GAMMA)
        for slot in range(slots):
            cut = lengths_ref[0:1, slot : slot + 1]
            row = lax.broadcasted_iota(jnp.int32, (tokens, 1), 0) < cut
            scale = jnp.where(
                row,
                factor[:, 2 * slot : 2 * slot + 1],
                factor[:, 2 * slot + 1 : 2 * slot + 2],
            )
            rows = slice(slot * tokens, (slot + 1) * tokens)
            dzc_ref[rows, :] = (dz[slot][...].astype(F32) * scale).astype(BF16)
            dyc_ref[rows, :] = (dy[slot][...].astype(F32) * scale).astype(BF16)

    block = grad_in_ref.shape[0]
    strip = pl.ds(pl.multiple_of(step * block, block), block)
    for left, right_ref, out_ref in ((x, dzc_ref, grad_in_ref), (hidden, dyc_ref, grad_out_ref)):
        for cols in parts(right_ref.shape[1]):
            total = tn(left[0][:, strip], right_ref[:tokens, cols])
            for slot in range(1, slots):
                rows = slice(slot * tokens, (slot + 1) * tokens)
                total = total + tn(left[slot][:, strip], right_ref[rows, cols])
            out_ref[:, cols] = total.astype(BF16)


def final_products(lengths, totals, x, hidden, dz, dy):
    slots = len(dz)
    tokens, width = dz[0].shape
    rows = x[0].shape[1]
    block = 256
    out = pl.BlockSpec((block, width), lambda i: (i, 0))
    return pl.pallas_call(
        lambda *refs: final_kernel(slots, *refs),
        grid=(rows // block,),
        out_shape=(shape(rows, width), shape(rows, width)),
        in_specs=[VMEM] * (2 + 4 * slots),
        out_specs=(out, out),
        scratch_shapes=[pltpu.VMEM((slots * tokens, width), BF16)] * 2,
        name="final",
        compiler_params=pltpu.CompilerParams(vmem_limit_bytes=12 * MIB),
        cost_estimate=pl.CostEstimate(
            flops=4 * rows * width * slots * tokens, bytes_accessed=4 * MIB, transcendentals=0
        ),
    )(lengths, totals, *x, *hidden, *dz, *dy)


def exchange(blocks):
    return lax.all_to_all(blocks, "tensor", split_axis=0, concat_axis=0, tiled=True)


def exchange_along_z(blocks):
    count = lax.axis_size("tensor")
    groups = [list(range(x, count, ALONG_X)) for x in range(ALONG_X)]
    return lax.all_to_all(
        blocks, "tensor", split_axis=0, concat_axis=0, axis_index_groups=groups, tiled=True
    )


def moved(value, sections_back, distance):
    sections, count = lax.axis_size("section"), lax.axis_size("tensor")
    pairs = [
        (
            section * count + at,
            (section - sections_back) % sections * count
            + at // ALONG_X * ALONG_X
            + (at + distance) % ALONG_X,
        )
        for section in range(sections)
        for at in range(count)
    ]
    return lax.ppermute(value, ("section", "tensor"), pairs)


def assemble(blocks):
    along_z, rows, width = blocks[0].shape
    outs = (shape(along_z, ALONG_X, rows, D),) * (width // D)
    gathered = call(assemble_kernel, outs, blocks, 0, "assemble")
    return [out.reshape(along_z * ALONG_X * rows, D) for out in gathered]


def per_device(saved_inputs, slot_index, example_lengths, first_grads, loss_grads, w_in, w_out):
    sections, count = lax.axis_size("section"), lax.axis_size("tensor")
    first, second = w_in[0], w_out[0]
    slots = loss_grads.shape[0] + 1
    rows = first_grads.shape[1]
    tokens = count * rows
    units = first.shape[1]
    lengths = example_lengths[0].T
    incoming = first_grads[0]
    product = 2 * tokens * D * units
    square = (tokens, tokens)

    along_z = count // ALONG_X
    blocks = pl.pallas_call(
        start_kernel,
        out_shape=shape(along_z, rows, (slots + 1) * D),
        in_specs=[pl.BlockSpec(memory_space=pl.ANY)] * 3,
        out_specs=VMEM,
        scratch_shapes=[
            pltpu.VMEM(slot_index.shape, jnp.int32),
            pltpu.VMEM(saved_inputs.shape[1:], BF16),
            pltpu.VMEM((rows, D), BF16),
            pltpu.SemaphoreType.DMA((3,)),
        ],
        name="start",
        compiler_params=pltpu.CompilerParams(vmem_limit_bytes=60 * MIB),
    )(slot_index, saved_inputs[0], incoming)
    begun = exchange_along_z(blocks)
    halves = (shape(along_z, rows, 2 * D), shape(along_z, rows, (slots - 1) * D))
    urgent, later = call(split_kernel, halves, (begun,), 0, "split")
    urgent, loss = lax.optimization_barrier((urgent, loss_grads))
    blocks = [urgent] + [moved(urgent, 0, distance) for distance in range(1, ALONG_X)]
    blocks[0], loss = lax.optimization_barrier((blocks[0], moved(loss, -1, 0)))
    x, grads = assemble(blocks)

    def forward(x):
        outs = (shape(tokens, units, dtype=F32), shape(tokens, units))
        return call(forward_kernel, outs, (x, first), product, "forward")

    slope, hidden = forward(x)
    xs, hiddens, dzs, dys, results, squares = [], [], [], [], [], []
    for slot in range(slots):
        xs.append(x)
        hiddens.append(hidden)
        dys.append(grads)
        if slot + 1 == slots:
            break
        dz, share = call(
            back_kernel,
            (shape(tokens, units), shape(tokens, D)),
            (grads, slope, second, first),
            2 * product,
            "back",
        )
        dzs.append(dz)
        arrived = exchange(share.reshape(count, rows, D))
        held = (x, hidden, grads, dz)
        if slot == 0:
            blocks = [later] + [moved(later, 0, distance) for distance in range(1, ALONG_X)]
            arrived, *later = lax.optimization_barrier((arrived, *assemble(blocks)))
        passing, blocks = call(
            lambda *refs, slot=slot: sum_kernel(slot, *refs),
            (shape(rows, D), shape(along_z, rows, D)),
            (arrived, grads.reshape(count, rows, D), loss),
            tokens * D,
            "add_up",
        )
        results.append(passing)
        block = exchange_along_z(blocks)
        pieces = [moved(block, 1, distance) for distance in range(ALONG_X)]
        *late, x = lax.optimization_barrier((block, *held, later[slot]))
        if slot:
            held = late[1:]
        one = call(
            lambda *refs, slot=slot: squares_kernel(slot, *refs),
            shape(1, LANES, dtype=F32),
            (lengths, *held),
            product,
            "squares",
        )
        squares.append(one)
        slope, hidden = forward(x)
        ready = [one, slope, hidden]
        if slot + 2 == slots:
            ready += call(
                grams_kernel, (shape(*square, dtype=F32),) * 2, (x, hidden), product // 4, "grams"
            )
        pieces[0], squares[-1], slope, hidden, *grams = lax.optimization_barrier(
            (pieces[0], *ready)
        )
        [grads] = assemble(pieces)

    dz, share = call(
        lambda *refs: last_back_kernel(slots - 1, *refs),
        (shape(tokens, units), shape(tokens, D + LANES)),
        (lengths, grads, slope, second, first, *grams, *squares),
        2 * product,
        "last_back",
    )
    dzs.append(dz)
    arrived = exchange(share.reshape(count, rows, D + LANES))
    results, totals = call(
        last_sum_kernel,
        (shape(slots, rows, D), shape(1, LANES, dtype=F32)),
        (arrived, grads.reshape(count, rows, D), *results),
        tokens * D,
        "last_add_up",
    )
    grad_in, grad_out = final_products(lengths, totals, xs, hiddens, dzs, dys)
    return grad_in[None], grad_out[None], results[None]


def solution(mesh):
    return jax.shard_map(
        per_device,
        mesh=mesh,
        in_specs=(
            P("section", None, "tensor", None),
            P("section", None),
            P("section", None, None),
            P("section", "tensor", None),
            P(None, "tensor", None),
            P("section", None, "tensor"),
            P("section", "tensor", None),
        ),
        out_specs=(
            P("section", None, "tensor"),
            P("section", "tensor", None),
            P("section", None, "tensor", None),
        ),
        check_vma=False,
    )
```

```python
import jax
import jax.numpy as jnp
from jax import lax
from jax.experimental import pallas as pl
from jax.experimental.pallas import tpu as pltpu
from jax.sharding import PartitionSpec as P

D = 1024
FF = 32768
GAMMA = 0.01
F32 = jnp.float32
BF16 = jnp.bfloat16
MIB = 1 << 20
STEP = 256
LANES = 128
SPACING = 32
ALONG_X = 4

VMEM = pl.BlockSpec(memory_space=pltpu.VMEM)


def shape(*dims, dtype=BF16):
    return jax.ShapeDtypeStruct(dims, dtype)


def call(kernel, outs, operands, flops, name):
    return pl.pallas_call(
        kernel,
        out_shape=outs,
        in_specs=[VMEM] * len(operands),
        out_specs=jax.tree.map(lambda _: VMEM, outs),
        name=name,
        compiler_params=pltpu.CompilerParams(vmem_limit_bytes=8 * MIB),
        cost_estimate=pl.CostEstimate(flops=flops, bytes_accessed=MIB, transcendentals=0),
    )(*operands)


def parts(extent):
    return [slice(at, at + STEP) for at in range(0, extent, STEP)]


def nt(a, b):
    return lax.dot_general(a, b, (((1,), (1,)), ((), ())), preferred_element_type=F32)


def tn(a, b):
    return lax.dot_general(a, b, (((0,), (0,)), ((), ())), preferred_element_type=F32)


def mm(a, b):
    return jnp.dot(a, b, preferred_element_type=F32)


def start_kernel(index, saved, grads, blocks_ref, index_v, saved_v, grads_v, sems):
    loads = [
        pltpu.make_async_copy(source, target, sems.at[place])
        for place, (source, target) in enumerate(
            ((index, index_v), (saved, saved_v), (grads, grads_v))
        )
    ]
    for load in loads:
        load.start()
    for load in loads:
        load.wait()
    count, rows, width = blocks_ref.shape
    for slot in range(index_v.shape[1]):
        wanted = index_v[:, slot : slot + 1]
        x = saved_v[0]
        for place in range(1, saved_v.shape[0]):
            x = jnp.where(wanted == place, saved_v[place], x)
        at = slot + 1 if slot else 0
        blocks_ref[:, :, D * at : D * (at + 1)] = jnp.broadcast_to(x[None], (count, rows, D))
    blocks_ref[:, :, D : 2 * D] = jnp.broadcast_to(grads_v[...][None], (count, rows, D))


def split_kernel(begun_ref, *out_refs):
    width = out_refs[0].shape[-1]
    for place, out_ref in enumerate(out_refs):
        out_ref[...] = begun_ref[:, :, width * place : width * (place + 1)]


def assemble_kernel(*refs):
    blocks, out_refs = refs[:ALONG_X], refs[ALONG_X:]
    mine = lax.axis_index("tensor") % ALONG_X
    for distance, block_ref in enumerate(blocks):
        source = (mine + (ALONG_X - distance)) % ALONG_X
        for place, out_ref in enumerate(out_refs):
            out_ref[:, pl.ds(source, 1)] = block_ref[:, :, D * place : D * (place + 1)][:, None]


def forward_kernel(x_ref, weights_ref, slope_ref, hidden_ref):
    x = x_ref[...]
    for cols in parts(weights_ref.shape[1]):
        relu = jnp.maximum(mm(x, weights_ref[:, cols]), 0.0)
        slope_ref[:, cols] = 2.0 * relu
        hidden_ref[:, cols] = (relu * relu).astype(BF16)


def masked_sums(slot, lengths_ref, paired):
    cut = lengths_ref[0:1, slot : slot + 1]
    tokens = paired.shape[0]
    row = lax.broadcasted_iota(jnp.int32, (tokens, tokens), 0) < cut
    col = lax.broadcasted_iota(jnp.int32, (tokens, tokens), 1) < cut
    before = jnp.sum(jnp.where(row & col, paired, 0.0), axis=(0, 1), keepdims=True)
    after = jnp.sum(jnp.where(row | col, 0.0, paired), axis=(0, 1), keepdims=True)
    lane = lax.broadcasted_iota(jnp.int32, (1, LANES), 1)
    return jnp.where(lane == 2 * slot, before, jnp.where(lane == 2 * slot + 1, after, 0.0))


def back_products(grads, slope_ref, w_out_ref, w_in_ref, dz_ref, share_ref):
    for part in parts(w_out_ref.shape[0]):
        back = nt(grads, w_out_ref[part, :])
        dz_ref[:, part] = (slope_ref[:, part] * back).astype(BF16)
    dz = dz_ref[...]
    for part in parts(w_in_ref.shape[0]):
        share_ref[:, part] = nt(dz, w_in_ref[part, :]).astype(BF16)
    return dz


def back_kernel(grads_ref, slope_ref, w_out_ref, w_in_ref, dz_ref, share_ref):
    back_products(grads_ref[...], slope_ref, w_out_ref, w_in_ref, dz_ref, share_ref)


def last_back_kernel(
    slot, lengths_ref, grads_ref, slope_ref, w_out_ref, w_in_ref, gram_x_ref, gram_h_ref, *refs
):
    *sums_refs, dz_ref, share_ref = refs
    grads = grads_ref[...]
    dz = back_products(grads, slope_ref, w_out_ref, w_in_ref, dz_ref, share_ref)
    paired = gram_x_ref[...] * nt(dz, dz) + gram_h_ref[...] * nt(grads, grads)
    total = masked_sums(slot, lengths_ref, paired)
    for sums_ref in sums_refs:
        total = total + sums_ref[...]
    high = total.astype(BF16)
    rest = total - high.astype(F32)
    middle = rest.astype(BF16)
    low = (rest - middle.astype(F32)).astype(BF16)
    line = high.astype(F32)
    for place, piece in ((1, middle), (2, low)):
        line = line + pltpu.roll(piece.astype(F32), place * SPACING, 1)
    share_ref[:, D:] = jnp.broadcast_to(line, (share_ref.shape[0], LANES)).astype(BF16)


def squares_kernel(slot, lengths_ref, x_ref, hidden_ref, grads_ref, dz_ref, sums_ref):
    x, hidden, grads, dz = x_ref[...], hidden_ref[...], grads_ref[...], dz_ref[...]
    paired = nt(x, x) * nt(dz, dz) + nt(hidden, hidden) * nt(grads, grads)
    sums_ref[...] = masked_sums(slot, lengths_ref, paired)


def grams_kernel(x_ref, hidden_ref, gram_x_ref, gram_h_ref):
    x, hidden = x_ref[...], hidden_ref[...]
    gram_x_ref[...] = nt(x, x)
    gram_h_ref[...] = nt(hidden, hidden)


def sum_kernel(place, arrived_ref, grads_ref, loss_ref, passing_ref, blocks_ref):
    total = grads_ref[lax.axis_index("tensor")].astype(F32)
    for peer in range(arrived_ref.shape[0]):
        total = total + arrived_ref[peer].astype(F32)
    passing = total.astype(BF16)
    passing_ref[...] = passing
    first = (lax.axis_index("section") == 0).astype(jnp.int32)
    chosen = jnp.where(jnp.full(passing.shape, first) > 0, loss_ref[place], passing)
    blocks_ref[...] = jnp.broadcast_to(chosen[None], blocks_ref.shape)


def last_sum_kernel(arrived_ref, grads_ref, *refs):
    *earlier_refs, results_ref, line_ref = refs
    total = grads_ref[lax.axis_index("tensor")].astype(F32)
    line = jnp.zeros(line_ref.shape, F32)
    for peer in range(arrived_ref.shape[0]):
        total = total + arrived_ref[peer, :, :D].astype(F32)
        line = line + arrived_ref[peer, 0:1, D:].astype(F32)
    for place, earlier_ref in enumerate(earlier_refs):
        results_ref[place] = earlier_ref[...]
    results_ref[len(earlier_refs)] = total.astype(BF16)
    pieces = [pltpu.roll(line, LANES - place * SPACING, 1) for place in (1, 2)]
    line_ref[...] = line + (pieces[0] + pieces[1])


def final_kernel(slots, lengths_ref, totals_ref, *refs):
    x, hidden, dz, dy = (refs[i * slots : (i + 1) * slots] for i in range(4))
    grad_in_ref, grad_out_ref, dzc_ref, dyc_ref = refs[4 * slots :]
    tokens = dz[0].shape[0]
    step = pl.program_id(0)

    @pl.when(step == 0)
    def _():
        factor = 1.0 / (jnp.sqrt(totals_ref[...] / (D * FF)) + GAMMA)
        for slot in range(slots):
            cut = lengths_ref[0:1, slot : slot + 1]
            row = lax.broadcasted_iota(jnp.int32, (tokens, 1), 0) < cut
            scale = jnp.where(
                row,
                factor[:, 2 * slot : 2 * slot + 1],
                factor[:, 2 * slot + 1 : 2 * slot + 2],
            )
            rows = slice(slot * tokens, (slot + 1) * tokens)
            dzc_ref[rows, :] = (dz[slot][...].astype(F32) * scale).astype(BF16)
            dyc_ref[rows, :] = (dy[slot][...].astype(F32) * scale).astype(BF16)

    block = grad_in_ref.shape[0]
    strip = pl.ds(pl.multiple_of(step * block, block), block)
    for left, right_ref, out_ref in ((x, dzc_ref, grad_in_ref), (hidden, dyc_ref, grad_out_ref)):
        for cols in parts(right_ref.shape[1]):
            total = tn(left[0][:, strip], right_ref[:tokens, cols])
            for slot in range(1, slots):
                rows = slice(slot * tokens, (slot + 1) * tokens)
                total = total + tn(left[slot][:, strip], right_ref[rows, cols])
            out_ref[:, cols] = total.astype(BF16)


def final_products(lengths, totals, x, hidden, dz, dy):
    slots = len(dz)
    tokens, width = dz[0].shape
    rows = x[0].shape[1]
    block = 256
    out = pl.BlockSpec((block, width), lambda i: (i, 0))
    return pl.pallas_call(
        lambda *refs: final_kernel(slots, *refs),
        grid=(rows // block,),
        out_shape=(shape(rows, width), shape(rows, width)),
        in_specs=[VMEM] * (2 + 4 * slots),
        out_specs=(out, out),
        scratch_shapes=[pltpu.VMEM((slots * tokens, width), BF16)] * 2,
        name="final",
        compiler_params=pltpu.CompilerParams(vmem_limit_bytes=12 * MIB),
        cost_estimate=pl.CostEstimate(
            flops=4 * rows * width * slots * tokens, bytes_accessed=4 * MIB, transcendentals=0
        ),
    )(lengths, totals, *x, *hidden, *dz, *dy)


def exchange(blocks):
    return lax.all_to_all(blocks, "tensor", split_axis=0, concat_axis=0, tiled=True)


def exchange_along_z(blocks):
    count = lax.axis_size("tensor")
    groups = [list(range(x, count, ALONG_X)) for x in range(ALONG_X)]
    return lax.all_to_all(
        blocks, "tensor", split_axis=0, concat_axis=0, axis_index_groups=groups, tiled=True
    )


def moved(value, sections_back, distance):
    sections, count = lax.axis_size("section"), lax.axis_size("tensor")
    pairs = [
        (
            section * count + at,
            (section - sections_back) % sections * count
            + at // ALONG_X * ALONG_X
            + (at + distance) % ALONG_X,
        )
        for section in range(sections)
        for at in range(count)
    ]
    return lax.ppermute(value, ("section", "tensor"), pairs)


def assemble(blocks):
    along_z, rows, width = blocks[0].shape
    outs = (shape(along_z, ALONG_X, rows, D),) * (width // D)
    gathered = call(assemble_kernel, outs, blocks, 0, "assemble")
    return [out.reshape(along_z * ALONG_X * rows, D) for out in gathered]


def per_device(saved_inputs, slot_index, example_lengths, first_grads, loss_grads, w_in, w_out):
    sections, count = lax.axis_size("section"), lax.axis_size("tensor")
    first, second = w_in[0], w_out[0]
    slots = loss_grads.shape[0] + 1
    rows = first_grads.shape[1]
    tokens = count * rows
    units = first.shape[1]
    lengths = example_lengths[0].T
    incoming = first_grads[0]
    product = 2 * tokens * D * units
    square = (tokens, tokens)

    along_z = count // ALONG_X
    blocks = pl.pallas_call(
        start_kernel,
        out_shape=shape(along_z, rows, (slots + 1) * D),
        in_specs=[pl.BlockSpec(memory_space=pl.ANY)] * 3,
        out_specs=VMEM,
        scratch_shapes=[
            pltpu.VMEM(slot_index.shape, jnp.int32),
            pltpu.VMEM(saved_inputs.shape[1:], BF16),
            pltpu.VMEM((rows, D), BF16),
            pltpu.SemaphoreType.DMA((3,)),
        ],
        name="start",
        compiler_params=pltpu.CompilerParams(vmem_limit_bytes=60 * MIB),
    )(slot_index, saved_inputs[0], incoming)
    begun = exchange_along_z(blocks)
    halves = (shape(along_z, rows, 2 * D), shape(along_z, rows, (slots - 1) * D))
    urgent, later = call(split_kernel, halves, (begun,), 0, "split")
    urgent, loss = lax.optimization_barrier((urgent, loss_grads))
    blocks = [urgent] + [moved(urgent, 0, distance) for distance in range(1, ALONG_X)]
    blocks[0], loss = lax.optimization_barrier((blocks[0], moved(loss, -1, 0)))
    x, grads = assemble(blocks)

    def forward(x):
        outs = (shape(tokens, units, dtype=F32), shape(tokens, units))
        return call(forward_kernel, outs, (x, first), product, "forward")

    slope, hidden = forward(x)
    xs, hiddens, dzs, dys, results, squares = [], [], [], [], [], []
    for slot in range(slots):
        xs.append(x)
        hiddens.append(hidden)
        dys.append(grads)
        if slot + 1 == slots:
            break
        dz, share = call(
            back_kernel,
            (shape(tokens, units), shape(tokens, D)),
            (grads, slope, second, first),
            2 * product,
            "back",
        )
        dzs.append(dz)
        arrived = exchange(share.reshape(count, rows, D))
        held = (x, hidden, grads, dz)
        if slot == 0:
            blocks = [later] + [moved(later, 0, distance) for distance in range(1, ALONG_X)]
            later = assemble(blocks)
        passing, blocks = call(
            lambda *refs, slot=slot: sum_kernel(slot, *refs),
            (shape(rows, D), shape(along_z, rows, D)),
            (arrived, grads.reshape(count, rows, D), loss),
            tokens * D,
            "add_up",
        )
        results.append(passing)
        block = exchange_along_z(blocks)
        pieces = [moved(block, 1, distance) for distance in range(ALONG_X)]
        *late, x = lax.optimization_barrier((block, *held, later[slot]))
        if slot:
            held = late[1:]
        one = call(
            lambda *refs, slot=slot: squares_kernel(slot, *refs),
            shape(1, LANES, dtype=F32),
            (lengths, *held),
            product,
            "squares",
        )
        squares.append(one)
        slope, hidden = forward(x)
        ready = [one, slope, hidden]
        if slot + 2 == slots:
            ready += call(
                grams_kernel, (shape(*square, dtype=F32),) * 2, (x, hidden), product // 4, "grams"
            )
        pieces[0], squares[-1], slope, hidden, *grams = lax.optimization_barrier(
            (pieces[0], *ready)
        )
        [grads] = assemble(pieces)

    dz, share = call(
        lambda *refs: last_back_kernel(slots - 1, *refs),
        (shape(tokens, units), shape(tokens, D + LANES)),
        (lengths, grads, slope, second, first, *grams, *squares),
        2 * product,
        "last_back",
    )
    dzs.append(dz)
    arrived = exchange(share.reshape(count, rows, D + LANES))
    results, totals = call(
        last_sum_kernel,
        (shape(slots, rows, D), shape(1, LANES, dtype=F32)),
        (arrived, grads.reshape(count, rows, D), *results),
        tokens * D,
        "last_add_up",
    )
    grad_in, grad_out = final_products(lengths, totals, xs, hiddens, dzs, dys)
    return grad_in[None], grad_out[None], results[None]


def solution(mesh):
    return jax.shard_map(
        per_device,
        mesh=mesh,
        in_specs=(
            P("section", None, "tensor", None),
            P("section", None),
            P("section", None, None),
            P("section", "tensor", None),
            P(None, "tensor", None),
            P("section", None, "tensor"),
            P("section", "tensor", None),
        ),
        out_specs=(
            P("section", None, "tensor"),
            P("section", "tensor", None),
            P("section", None, "tensor", None),
        ),
        check_vma=False,
    )
```

```python
import jax
import jax.numpy as jnp
from jax import lax
from jax.experimental import pallas as pl
from jax.experimental.pallas import tpu as pltpu
from jax.sharding import PartitionSpec as P

D = 1024
FF = 32768
GAMMA = 0.01
F32 = jnp.float32
BF16 = jnp.bfloat16
MIB = 1 << 20
STEP = 256
LANES = 128
SPACING = 32
ALONG_X = 4

VMEM = pl.BlockSpec(memory_space=pltpu.VMEM)


def shape(*dims, dtype=BF16):
    return jax.ShapeDtypeStruct(dims, dtype)


def call(kernel, outs, operands, flops, name):
    return pl.pallas_call(
        kernel,
        out_shape=outs,
        in_specs=[VMEM] * len(operands),
        out_specs=jax.tree.map(lambda _: VMEM, outs),
        name=name,
        compiler_params=pltpu.CompilerParams(vmem_limit_bytes=8 * MIB),
        cost_estimate=pl.CostEstimate(flops=flops, bytes_accessed=MIB, transcendentals=0),
    )(*operands)


def parts(extent):
    return [slice(at, at + STEP) for at in range(0, extent, STEP)]


def nt(a, b):
    return lax.dot_general(a, b, (((1,), (1,)), ((), ())), preferred_element_type=F32)


def tn(a, b):
    return lax.dot_general(a, b, (((0,), (0,)), ((), ())), preferred_element_type=F32)


def mm(a, b):
    return jnp.dot(a, b, preferred_element_type=F32)


def start_kernel(index, saved, grads, blocks_ref, index_v, saved_v, grads_v, sems):
    loads = [
        pltpu.make_async_copy(source, target, sems.at[place])
        for place, (source, target) in enumerate(
            ((index, index_v), (saved, saved_v), (grads, grads_v))
        )
    ]
    for load in loads:
        load.start()
    for load in loads:
        load.wait()
    count, rows, width = blocks_ref.shape
    for slot in range(index_v.shape[1]):
        wanted = index_v[:, slot : slot + 1]
        x = saved_v[0]
        for place in range(1, saved_v.shape[0]):
            x = jnp.where(wanted == place, saved_v[place], x)
        at = slot + 1 if slot else 0
        blocks_ref[:, :, D * at : D * (at + 1)] = jnp.broadcast_to(x[None], (count, rows, D))
    blocks_ref[:, :, D : 2 * D] = jnp.broadcast_to(grads_v[...][None], (count, rows, D))


def split_kernel(begun_ref, *out_refs):
    width = out_refs[0].shape[-1]
    for place, out_ref in enumerate(out_refs):
        out_ref[...] = begun_ref[:, :, width * place : width * (place + 1)]


def assemble_kernel(*refs):
    blocks, out_refs = refs[:ALONG_X], refs[ALONG_X:]
    mine = lax.axis_index("tensor") % ALONG_X
    for distance, block_ref in enumerate(blocks):
        source = (mine + (ALONG_X - distance)) % ALONG_X
        for place, out_ref in enumerate(out_refs):
            out_ref[:, pl.ds(source, 1)] = block_ref[:, :, D * place : D * (place + 1)][:, None]


def forward_kernel(x_ref, weights_ref, slope_ref, hidden_ref):
    x = x_ref[...]
    for cols in parts(weights_ref.shape[1]):
        relu = jnp.maximum(mm(x, weights_ref[:, cols]), 0.0)
        slope_ref[:, cols] = 2.0 * relu
        hidden_ref[:, cols] = (relu * relu).astype(BF16)


def masked_sums(slot, lengths_ref, paired):
    cut = lengths_ref[0:1, slot : slot + 1]
    tokens = paired.shape[0]
    row = lax.broadcasted_iota(jnp.int32, (tokens, tokens), 0) < cut
    col = lax.broadcasted_iota(jnp.int32, (tokens, tokens), 1) < cut
    before = jnp.sum(jnp.where(row & col, paired, 0.0), axis=(0, 1), keepdims=True)
    after = jnp.sum(jnp.where(row | col, 0.0, paired), axis=(0, 1), keepdims=True)
    lane = lax.broadcasted_iota(jnp.int32, (1, LANES), 1)
    return jnp.where(lane == 2 * slot, before, jnp.where(lane == 2 * slot + 1, after, 0.0))


def back_products(grads, slope_ref, w_out_ref, w_in_ref, dz_ref, share_ref):
    for part in parts(w_out_ref.shape[0]):
        back = nt(grads, w_out_ref[part, :])
        dz_ref[:, part] = (slope_ref[:, part] * back).astype(BF16)
    dz = dz_ref[...]
    for part in parts(w_in_ref.shape[0]):
        share_ref[:, part] = nt(dz, w_in_ref[part, :]).astype(BF16)
    return dz


def back_kernel(grads_ref, slope_ref, w_out_ref, w_in_ref, dz_ref, share_ref):
    back_products(grads_ref[...], slope_ref, w_out_ref, w_in_ref, dz_ref, share_ref)


def last_back_kernel(
    slot, lengths_ref, grads_ref, slope_ref, w_out_ref, w_in_ref, gram_x_ref, gram_h_ref, *refs
):
    *sums_refs, dz_ref, share_ref = refs
    grads = grads_ref[...]
    dz = back_products(grads, slope_ref, w_out_ref, w_in_ref, dz_ref, share_ref)
    paired = gram_x_ref[...] * nt(dz, dz) + gram_h_ref[...] * nt(grads, grads)
    total = masked_sums(slot, lengths_ref, paired)
    for sums_ref in sums_refs:
        total = total + sums_ref[...]
    high = total.astype(BF16)
    rest = total - high.astype(F32)
    middle = rest.astype(BF16)
    low = (rest - middle.astype(F32)).astype(BF16)
    line = high.astype(F32)
    for place, piece in ((1, middle), (2, low)):
        line = line + pltpu.roll(piece.astype(F32), place * SPACING, 1)
    share_ref[:, D:] = jnp.broadcast_to(line, (share_ref.shape[0], LANES)).astype(BF16)


def squares_kernel(slot, lengths_ref, x_ref, hidden_ref, grads_ref, dz_ref, sums_ref):
    x, hidden, grads, dz = x_ref[...], hidden_ref[...], grads_ref[...], dz_ref[...]
    paired = nt(x, x) * nt(dz, dz) + nt(hidden, hidden) * nt(grads, grads)
    sums_ref[...] = masked_sums(slot, lengths_ref, paired)


def grams_kernel(x_ref, hidden_ref, gram_x_ref, gram_h_ref):
    x, hidden = x_ref[...], hidden_ref[...]
    gram_x_ref[...] = nt(x, x)
    gram_h_ref[...] = nt(hidden, hidden)


def sum_kernel(place, arrived_ref, grads_ref, loss_ref, passing_ref, blocks_ref):
    total = grads_ref[lax.axis_index("tensor")].astype(F32)
    for peer in range(arrived_ref.shape[0]):
        total = total + arrived_ref[peer].astype(F32)
    passing = total.astype(BF16)
    passing_ref[...] = passing
    first = (lax.axis_index("section") == 0).astype(jnp.int32)
    chosen = jnp.where(jnp.full(passing.shape, first) > 0, loss_ref[place], passing)
    blocks_ref[...] = jnp.broadcast_to(chosen[None], blocks_ref.shape)


def final_kernel(slots, lengths_ref, arrived_ref, own_ref, *refs):
    earlier_refs, refs = refs[: slots - 1], refs[slots - 1 :]
    x, hidden, dz, dy = (refs[i * slots : (i + 1) * slots] for i in range(4))
    grad_in_ref, grad_out_ref, results_ref, dzc_ref, dyc_ref = refs[4 * slots :]
    tokens = dz[0].shape[0]
    step = pl.program_id(0)

    @pl.when(step == 0)
    def _():
        total = own_ref[lax.axis_index("tensor")].astype(F32)
        line = jnp.zeros((1, LANES), F32)
        for peer in range(arrived_ref.shape[0]):
            total = total + arrived_ref[peer, :, :D].astype(F32)
            line = line + arrived_ref[peer, 0:1, D:].astype(F32)
        for place, earlier_ref in enumerate(earlier_refs):
            results_ref[place] = earlier_ref[...]
        results_ref[slots - 1] = total.astype(BF16)
        pieces = [pltpu.roll(line, LANES - place * SPACING, 1) for place in (1, 2)]
        squares = line + (pieces[0] + pieces[1])
        factor = 1.0 / (jnp.sqrt(squares / (D * FF)) + GAMMA)
        for slot in range(slots):
            cut = lengths_ref[0:1, slot : slot + 1]
            row = lax.broadcasted_iota(jnp.int32, (tokens, 1), 0) < cut
            scale = jnp.where(
                row,
                factor[:, 2 * slot : 2 * slot + 1],
                factor[:, 2 * slot + 1 : 2 * slot + 2],
            )
            rows = slice(slot * tokens, (slot + 1) * tokens)
            dzc_ref[rows, :] = (dz[slot][...].astype(F32) * scale).astype(BF16)
            dyc_ref[rows, :] = (dy[slot][...].astype(F32) * scale).astype(BF16)

    block = grad_in_ref.shape[0]
    strip = pl.ds(pl.multiple_of(step * block, block), block)
    for left, right_ref, out_ref in ((x, dzc_ref, grad_in_ref), (hidden, dyc_ref, grad_out_ref)):
        lhs = jnp.concatenate([part[:, strip] for part in left], axis=0)
        for cols in parts(right_ref.shape[1]):
            out_ref[:, cols] = tn(lhs, right_ref[:, cols]).astype(BF16)


def final_products(lengths, arrived, own, earlier, x, hidden, dz, dy):
    slots = len(dz)
    tokens, width = dz[0].shape
    rows = x[0].shape[1]
    block = 512
    out = pl.BlockSpec((block, width), lambda i: (i, 0))
    results = shape(slots, *earlier[0].shape)
    return pl.pallas_call(
        lambda *refs: final_kernel(slots, *refs),
        grid=(rows // block,),
        out_shape=(shape(rows, width), shape(rows, width), results),
        in_specs=[VMEM] * (3 + slots - 1 + 4 * slots),
        out_specs=(out, out, pl.BlockSpec(results.shape, lambda i: (0, 0, 0))),
        scratch_shapes=[pltpu.VMEM((slots * tokens, width), BF16)] * 2,
        name="final",
        compiler_params=pltpu.CompilerParams(vmem_limit_bytes=16 * MIB),
        cost_estimate=pl.CostEstimate(
            flops=4 * rows * width * slots * tokens, bytes_accessed=4 * MIB, transcendentals=0
        ),
    )(lengths, arrived, own, *earlier, *x, *hidden, *dz, *dy)


def exchange(blocks):
    return lax.all_to_all(blocks, "tensor", split_axis=0, concat_axis=0, tiled=True)


def exchange_along_z(blocks):
    count = lax.axis_size("tensor")
    groups = [list(range(x, count, ALONG_X)) for x in range(ALONG_X)]
    return lax.all_to_all(
        blocks, "tensor", split_axis=0, concat_axis=0, axis_index_groups=groups, tiled=True
    )


def moved(value, sections_back, distance):
    sections, count = lax.axis_size("section"), lax.axis_size("tensor")
    pairs = [
        (
            section * count + at,
            (section - sections_back) % sections * count
            + at // ALONG_X * ALONG_X
            + (at + distance) % ALONG_X,
        )
        for section in range(sections)
        for at in range(count)
    ]
    return lax.ppermute(value, ("section", "tensor"), pairs)


def assemble(blocks):
    along_z, rows, width = blocks[0].shape
    outs = (shape(along_z, ALONG_X, rows, D),) * (width // D)
    gathered = call(assemble_kernel, outs, blocks, 0, "assemble")
    return [out.reshape(along_z * ALONG_X * rows, D) for out in gathered]


def per_device(saved_inputs, slot_index, example_lengths, first_grads, loss_grads, w_in, w_out):
    sections, count = lax.axis_size("section"), lax.axis_size("tensor")
    first, second = w_in[0], w_out[0]
    slots = loss_grads.shape[0] + 1
    rows = first_grads.shape[1]
    tokens = count * rows
    units = first.shape[1]
    lengths = example_lengths[0].T
    incoming = first_grads[0]
    product = 2 * tokens * D * units
    square = (tokens, tokens)

    along_z = count // ALONG_X
    blocks = pl.pallas_call(
        start_kernel,
        out_shape=shape(along_z, rows, (slots + 1) * D),
        in_specs=[pl.BlockSpec(memory_space=pl.ANY)] * 3,
        out_specs=VMEM,
        scratch_shapes=[
            pltpu.VMEM(slot_index.shape, jnp.int32),
            pltpu.VMEM(saved_inputs.shape[1:], BF16),
            pltpu.VMEM((rows, D), BF16),
            pltpu.SemaphoreType.DMA((3,)),
        ],
        name="start",
        compiler_params=pltpu.CompilerParams(vmem_limit_bytes=60 * MIB),
    )(slot_index, saved_inputs[0], incoming)
    begun = exchange_along_z(blocks)
    halves = (shape(along_z, rows, 2 * D), shape(along_z, rows, (slots - 1) * D))
    urgent, later = call(split_kernel, halves, (begun,), 0, "split")
    urgent, loss = lax.optimization_barrier((urgent, loss_grads))
    blocks = [urgent] + [moved(urgent, 0, distance) for distance in range(1, ALONG_X)]
    blocks[0], loss = lax.optimization_barrier((blocks[0], moved(loss, -1, 0)))
    x, grads = assemble(blocks)

    def forward(x):
        outs = (shape(tokens, units, dtype=F32), shape(tokens, units))
        return call(forward_kernel, outs, (x, first), product, "forward")

    slope, hidden = forward(x)
    xs, hiddens, dzs, dys, results, squares = [], [], [], [], [], []
    for slot in range(slots):
        xs.append(x)
        hiddens.append(hidden)
        dys.append(grads)
        if slot + 1 == slots:
            break
        dz, share = call(
            back_kernel,
            (shape(tokens, units), shape(tokens, D)),
            (grads, slope, second, first),
            2 * product,
            "back",
        )
        dzs.append(dz)
        arrived = exchange(share.reshape(count, rows, D))
        held = (x, hidden, grads, dz)
        if slot == 0:
            blocks = [later] + [moved(later, 0, distance) for distance in range(1, ALONG_X)]
            later = assemble(blocks)
        passing, blocks = call(
            lambda *refs, slot=slot: sum_kernel(slot, *refs),
            (shape(rows, D), shape(along_z, rows, D)),
            (arrived, grads.reshape(count, rows, D), loss),
            tokens * D,
            "add_up",
        )
        results.append(passing)
        block = exchange_along_z(blocks)
        pieces = [moved(block, 1, distance) for distance in range(ALONG_X)]
        *late, x = lax.optimization_barrier((block, *held, later[slot]))
        if slot:
            held = late[1:]
        one = call(
            lambda *refs, slot=slot: squares_kernel(slot, *refs),
            shape(1, LANES, dtype=F32),
            (lengths, *held),
            product,
            "squares",
        )
        squares.append(one)
        slope, hidden = forward(x)
        ready = [one, slope, hidden]
        if slot + 2 == slots:
            ready += call(
                grams_kernel, (shape(*square, dtype=F32),) * 2, (x, hidden), product // 4, "grams"
            )
        pieces[0], squares[-1], slope, hidden, *grams = lax.optimization_barrier(
            (pieces[0], *ready)
        )
        [grads] = assemble(pieces)

    dz, share = call(
        lambda *refs: last_back_kernel(slots - 1, *refs),
        (shape(tokens, units), shape(tokens, D + LANES)),
        (lengths, grads, slope, second, first, *grams, *squares),
        2 * product,
        "last_back",
    )
    dzs.append(dz)
    arrived = exchange(share.reshape(count, rows, D + LANES))
    own = grads.reshape(count, rows, D)
    grad_in, grad_out, results = final_products(
        lengths, arrived, own, results, xs, hiddens, dzs, dys
    )
    return grad_in[None], grad_out[None], results[None]


def solution(mesh):
    return jax.shard_map(
        per_device,
        mesh=mesh,
        in_specs=(
            P("section", None, "tensor", None),
            P("section", None),
            P("section", None, None),
            P("section", "tensor", None),
            P(None, "tensor", None),
            P("section", None, "tensor"),
            P("section", "tensor", None),
        ),
        out_specs=(
            P("section", None, "tensor"),
            P("section", "tensor", None),
            P("section", None, "tensor", None),
        ),
        check_vma=False,
    )
```

```python
import jax
import jax.numpy as jnp
from jax import lax
from jax.experimental import pallas as pl
from jax.experimental.pallas import tpu as pltpu
from jax.sharding import PartitionSpec as P

D = 1024
FF = 32768
GAMMA = 0.01
F32 = jnp.float32
BF16 = jnp.bfloat16
MIB = 1 << 20
STEP = 256
LANES = 128
SPACING = 32
ALONG_X = 4

VMEM = pl.BlockSpec(memory_space=pltpu.VMEM)


def shape(*dims, dtype=BF16):
    return jax.ShapeDtypeStruct(dims, dtype)


def call(kernel, outs, operands, flops, name, scratch=()):
    return pl.pallas_call(
        kernel,
        out_shape=outs,
        in_specs=[VMEM] * len(operands),
        out_specs=jax.tree.map(lambda _: VMEM, outs),
        scratch_shapes=[pltpu.VMEM(dims, BF16) for dims in scratch],
        name=name,
        compiler_params=pltpu.CompilerParams(vmem_limit_bytes=8 * MIB),
        cost_estimate=pl.CostEstimate(flops=flops, bytes_accessed=MIB, transcendentals=0),
    )(*operands)


def parts(extent):
    return [slice(at, at + STEP) for at in range(0, extent, STEP)]


def nt(a, b):
    return lax.dot_general(a, b, (((1,), (1,)), ((), ())), preferred_element_type=F32)


def tn(a, b):
    return lax.dot_general(a, b, (((0,), (0,)), ((), ())), preferred_element_type=F32)


def mm(a, b):
    return jnp.dot(a, b, preferred_element_type=F32)


def start_kernel(index, saved, grads, blocks_ref, index_v, saved_v, grads_v, sems):
    loads = [
        pltpu.make_async_copy(source, target, sems.at[place])
        for place, (source, target) in enumerate(
            ((index, index_v), (saved, saved_v), (grads, grads_v))
        )
    ]
    for load in loads:
        load.start()
    for load in loads:
        load.wait()
    count, rows, width = blocks_ref.shape
    for slot in range(index_v.shape[1]):
        wanted = index_v[:, slot : slot + 1]
        x = saved_v[0]
        for place in range(1, saved_v.shape[0]):
            x = jnp.where(wanted == place, saved_v[place], x)
        at = slot + 1 if slot else 0
        blocks_ref[:, :, D * at : D * (at + 1)] = jnp.broadcast_to(x[None], (count, rows, D))
    blocks_ref[:, :, D : 2 * D] = jnp.broadcast_to(grads_v[...][None], (count, rows, D))


def split_kernel(begun_ref, *out_refs):
    width = out_refs[0].shape[-1]
    for place, out_ref in enumerate(out_refs):
        out_ref[...] = begun_ref[:, :, width * place : width * (place + 1)]


def assemble_kernel(*refs):
    blocks, out_refs = refs[:ALONG_X], refs[ALONG_X:]
    mine = lax.axis_index("tensor") % ALONG_X
    for distance, block_ref in enumerate(blocks):
        source = (mine + (ALONG_X - distance)) % ALONG_X
        for place, out_ref in enumerate(out_refs):
            out_ref[:, pl.ds(source, 1)] = block_ref[:, :, D * place : D * (place + 1)][:, None]


def forward_kernel(x_ref, weights_ref, slope_ref, hidden_ref):
    x = x_ref[...]
    for cols in parts(weights_ref.shape[1]):
        relu = jnp.maximum(mm(x, weights_ref[:, cols]), 0.0)
        slope_ref[:, cols] = 2.0 * relu
        hidden_ref[:, cols] = (relu * relu).astype(BF16)


def slope_kernel(x_ref, weights_ref, slope_ref):
    x = x_ref[...]
    for cols in parts(weights_ref.shape[1]):
        slope_ref[:, cols] = 2.0 * jnp.maximum(mm(x, weights_ref[:, cols]), 0.0)


def again_kernel(x_ref, grads_ref, w_in_ref, w_out_ref, hidden_ref, dz_ref):
    x, grads = x_ref[...], grads_ref[...]
    for part in parts(w_in_ref.shape[1]):
        relu = jnp.maximum(mm(x, w_in_ref[:, part]), 0.0)
        hidden_ref[:, part] = (relu * relu).astype(BF16)
        dz_ref[:, part] = (2.0 * relu * nt(grads, w_out_ref[part, :])).astype(BF16)


def masked_sums(slot, lengths_ref, paired):
    cut = lengths_ref[0:1, slot : slot + 1]
    tokens = paired.shape[0]
    row = lax.broadcasted_iota(jnp.int32, (tokens, tokens), 0) < cut
    col = lax.broadcasted_iota(jnp.int32, (tokens, tokens), 1) < cut
    before = jnp.sum(jnp.where(row & col, paired, 0.0), axis=(0, 1), keepdims=True)
    after = jnp.sum(jnp.where(row | col, 0.0, paired), axis=(0, 1), keepdims=True)
    lane = lax.broadcasted_iota(jnp.int32, (1, LANES), 1)
    return jnp.where(lane == 2 * slot, before, jnp.where(lane == 2 * slot + 1, after, 0.0))


def back_products(grads, slope_ref, w_out_ref, w_in_ref, dz_ref, share_ref):
    for part in parts(w_out_ref.shape[0]):
        back = nt(grads, w_out_ref[part, :])
        dz_ref[:, part] = (slope_ref[:, part] * back).astype(BF16)
    dz = dz_ref[...]
    for part in parts(w_in_ref.shape[0]):
        share_ref[:, part] = nt(dz, w_in_ref[part, :]).astype(BF16)
    return dz


def back_kernel(grads_ref, slope_ref, w_out_ref, w_in_ref, dz_ref, share_ref):
    back_products(grads_ref[...], slope_ref, w_out_ref, w_in_ref, dz_ref, share_ref)


def first_back_kernel(grads_ref, slope_ref, w_out_ref, w_in_ref, share_ref, dz_ref):
    back_products(grads_ref[...], slope_ref, w_out_ref, w_in_ref, dz_ref, share_ref)


def last_back_kernel(
    slot, lengths_ref, grads_ref, slope_ref, w_out_ref, w_in_ref, gram_x_ref, gram_h_ref, *refs
):
    *sums_refs, dz_ref, share_ref = refs
    grads = grads_ref[...]
    dz = back_products(grads, slope_ref, w_out_ref, w_in_ref, dz_ref, share_ref)
    paired = gram_x_ref[...] * nt(dz, dz) + gram_h_ref[...] * nt(grads, grads)
    total = masked_sums(slot, lengths_ref, paired)
    for sums_ref in sums_refs:
        total = total + sums_ref[...]
    high = total.astype(BF16)
    rest = total - high.astype(F32)
    middle = rest.astype(BF16)
    low = (rest - middle.astype(F32)).astype(BF16)
    line = high.astype(F32)
    for place, piece in ((1, middle), (2, low)):
        line = line + pltpu.roll(piece.astype(F32), place * SPACING, 1)
    share_ref[:, D:] = jnp.broadcast_to(line, (share_ref.shape[0], LANES)).astype(BF16)


def squares_kernel(slot, lengths_ref, x_ref, hidden_ref, grads_ref, dz_ref, sums_ref):
    x, hidden, grads, dz = x_ref[...], hidden_ref[...], grads_ref[...], dz_ref[...]
    paired = nt(x, x) * nt(dz, dz) + nt(hidden, hidden) * nt(grads, grads)
    sums_ref[...] = masked_sums(slot, lengths_ref, paired)


def grams_kernel(x_ref, hidden_ref, gram_x_ref, gram_h_ref):
    x, hidden = x_ref[...], hidden_ref[...]
    gram_x_ref[...] = nt(x, x)
    gram_h_ref[...] = nt(hidden, hidden)


def sum_kernel(place, arrived_ref, grads_ref, loss_ref, passing_ref, blocks_ref):
    own = lax.axis_index("tensor") if grads_ref.shape[0] > 1 else 0
    total = grads_ref[own].astype(F32)
    for peer in range(arrived_ref.shape[0]):
        total = total + arrived_ref[peer].astype(F32)
    passing = total.astype(BF16)
    passing_ref[...] = passing
    first = (lax.axis_index("section") == 0).astype(jnp.int32)
    chosen = jnp.where(jnp.full(passing.shape, first) > 0, loss_ref[place], passing)
    blocks_ref[...] = jnp.broadcast_to(chosen[None], blocks_ref.shape)


def final_kernel(slots, lengths_ref, arrived_ref, own_ref, *refs):
    earlier_refs, refs = refs[: slots - 1], refs[slots - 1 :]
    x, hidden, dz, dy = (refs[i * slots : (i + 1) * slots] for i in range(4))
    grad_in_ref, grad_out_ref, results_ref, dzc_ref, dyc_ref = refs[4 * slots :]
    tokens = dz[0].shape[0]
    step = pl.program_id(0)

    @pl.when(step == 0)
    def _():
        total = own_ref[lax.axis_index("tensor")].astype(F32)
        line = jnp.zeros((1, LANES), F32)
        for peer in range(arrived_ref.shape[0]):
            total = total + arrived_ref[peer, :, :D].astype(F32)
            line = line + arrived_ref[peer, 0:1, D:].astype(F32)
        for place, earlier_ref in enumerate(earlier_refs):
            results_ref[place] = earlier_ref[...]
        results_ref[slots - 1] = total.astype(BF16)
        pieces = [pltpu.roll(line, LANES - place * SPACING, 1) for place in (1, 2)]
        squares = line + (pieces[0] + pieces[1])
        factor = 1.0 / (jnp.sqrt(squares / (D * FF)) + GAMMA)
        for slot in range(slots):
            cut = lengths_ref[0:1, slot : slot + 1]
            row = lax.broadcasted_iota(jnp.int32, (tokens, 1), 0) < cut
            scale = jnp.where(
                row,
                factor[:, 2 * slot : 2 * slot + 1],
                factor[:, 2 * slot + 1 : 2 * slot + 2],
            )
            rows = slice(slot * tokens, (slot + 1) * tokens)
            dzc_ref[rows, :] = (dz[slot][...].astype(F32) * scale).astype(BF16)
            dyc_ref[rows, :] = (dy[slot][...].astype(F32) * scale).astype(BF16)

    block = grad_in_ref.shape[0]
    strip = pl.ds(pl.multiple_of(step * block, block), block)
    for left, right_ref, out_ref in ((x, dzc_ref, grad_in_ref), (hidden, dyc_ref, grad_out_ref)):
        lhs = jnp.concatenate([part[:, strip] for part in left], axis=0)
        for cols in parts(right_ref.shape[1]):
            out_ref[:, cols] = tn(lhs, right_ref[:, cols]).astype(BF16)


def final_products(lengths, arrived, own, earlier, x, hidden, dz, dy):
    slots = len(dz)
    tokens, width = dz[0].shape
    rows = x[0].shape[1]
    block = 512
    out = pl.BlockSpec((block, width), lambda i: (i, 0))
    results = shape(slots, *earlier[0].shape)
    return pl.pallas_call(
        lambda *refs: final_kernel(slots, *refs),
        grid=(rows // block,),
        out_shape=(shape(rows, width), shape(rows, width), results),
        in_specs=[VMEM] * (3 + slots - 1 + 4 * slots),
        out_specs=(out, out, pl.BlockSpec(results.shape, lambda i: (0, 0, 0))),
        scratch_shapes=[pltpu.VMEM((slots * tokens, width), BF16)] * 2,
        name="final",
        compiler_params=pltpu.CompilerParams(vmem_limit_bytes=16 * MIB),
        cost_estimate=pl.CostEstimate(
            flops=4 * rows * width * slots * tokens, bytes_accessed=4 * MIB, transcendentals=0
        ),
    )(lengths, arrived, own, *earlier, *x, *hidden, *dz, *dy)


def exchange(blocks):
    return lax.all_to_all(blocks, "tensor", split_axis=0, concat_axis=0, tiled=True)


def exchange_along_z(blocks):
    count = lax.axis_size("tensor")
    groups = [list(range(x, count, ALONG_X)) for x in range(ALONG_X)]
    return lax.all_to_all(
        blocks, "tensor", split_axis=0, concat_axis=0, axis_index_groups=groups, tiled=True
    )


def moved(value, sections_back, distance):
    sections, count = lax.axis_size("section"), lax.axis_size("tensor")
    pairs = [
        (
            section * count + at,
            (section - sections_back) % sections * count
            + at // ALONG_X * ALONG_X
            + (at + distance) % ALONG_X,
        )
        for section in range(sections)
        for at in range(count)
    ]
    return lax.ppermute(value, ("section", "tensor"), pairs)


def assemble(blocks):
    along_z, rows, width = blocks[0].shape
    outs = (shape(along_z, ALONG_X, rows, D),) * (width // D)
    gathered = call(assemble_kernel, outs, blocks, 0, "assemble")
    return [out.reshape(along_z * ALONG_X * rows, D) for out in gathered]


def per_device(saved_inputs, slot_index, example_lengths, first_grads, loss_grads, w_in, w_out):
    sections, count = lax.axis_size("section"), lax.axis_size("tensor")
    first, second = w_in[0], w_out[0]
    slots = loss_grads.shape[0] + 1
    rows = first_grads.shape[1]
    tokens = count * rows
    units = first.shape[1]
    lengths = example_lengths[0].T
    incoming = first_grads[0]
    product = 2 * tokens * D * units
    square = (tokens, tokens)

    along_z = count // ALONG_X
    blocks = pl.pallas_call(
        start_kernel,
        out_shape=shape(along_z, rows, (slots + 1) * D),
        in_specs=[pl.BlockSpec(memory_space=pl.ANY)] * 3,
        out_specs=VMEM,
        scratch_shapes=[
            pltpu.VMEM(slot_index.shape, jnp.int32),
            pltpu.VMEM(saved_inputs.shape[1:], BF16),
            pltpu.VMEM((rows, D), BF16),
            pltpu.SemaphoreType.DMA((3,)),
        ],
        name="start",
        compiler_params=pltpu.CompilerParams(vmem_limit_bytes=60 * MIB),
    )(slot_index, saved_inputs[0], incoming)
    begun = exchange_along_z(blocks)
    halves = (shape(along_z, rows, 2 * D), shape(along_z, rows, (slots - 1) * D))
    urgent, later = call(split_kernel, halves, (begun,), 0, "split")
    urgent, loss = lax.optimization_barrier((urgent, loss_grads))
    blocks = [urgent] + [moved(urgent, 0, distance) for distance in range(1, ALONG_X)]
    blocks[0], loss = lax.optimization_barrier((blocks[0], moved(loss, -1, 0)))
    x, grads = assemble(blocks)

    def forward(x):
        outs = (shape(tokens, units, dtype=F32), shape(tokens, units))
        return call(forward_kernel, outs, (x, first), product, "forward")

    slope = call(
        slope_kernel, shape(tokens, units, dtype=F32), (x, first), product, "slope"
    )
    xs, hiddens, dzs, dys, results, squares = [], [], [], [], [], []
    for slot in range(slots - 1):
        if slot:
            dz, share = call(
                back_kernel,
                (shape(tokens, units), shape(tokens, D)),
                (grads, slope, second, first),
                2 * product,
                "back",
            )
            own = grads.reshape(count, rows, D)
        else:
            share = call(
                first_back_kernel,
                shape(tokens, D),
                (grads, slope, second, first),
                2 * product,
                "first_back",
                scratch=[(tokens, units)],
            )
            own = first_grads
        arrived = exchange(share.reshape(count, rows, D))
        if slot == 0:
            blocks = [later] + [moved(later, 0, distance) for distance in range(1, ALONG_X)]
            later = assemble(blocks)
        passing, blocks = call(
            lambda *refs, slot=slot: sum_kernel(slot, *refs),
            (shape(rows, D), shape(along_z, rows, D)),
            (arrived, own, loss),
            tokens * D,
            "add_up",
        )
        results.append(passing)
        block = exchange_along_z(blocks)
        pieces = [moved(block, 1, distance) for distance in range(ALONG_X)]
        made = (hidden, dz) if slot else (first, second)
        _, next_x, x, grads, *made = lax.optimization_barrier(
            (block, later[slot], x, grads, *made)
        )
        if slot:
            hidden, dz = made
        else:
            hidden, dz = call(
                again_kernel, (shape(tokens, units),) * 2, (x, grads, *made), 0, "again"
            )
        for kept, value in ((xs, x), (hiddens, hidden), (dzs, dz), (dys, grads)):
            kept.append(value)
        one = call(
            lambda *refs, slot=slot: squares_kernel(slot, *refs),
            shape(1, LANES, dtype=F32),
            (lengths, x, hidden, grads, dz),
            product,
            "squares",
        )
        x = next_x
        squares.append(one)
        slope, hidden = forward(x)
        ready = [one, slope, hidden]
        if slot + 2 == slots:
            ready += call(
                grams_kernel, (shape(*square, dtype=F32),) * 2, (x, hidden), product // 4, "grams"
            )
        pieces[0], squares[-1], slope, hidden, *grams = lax.optimization_barrier(
            (pieces[0], *ready)
        )
        [grads] = assemble(pieces)

    dz, share = call(
        lambda *refs: last_back_kernel(slots - 1, *refs),
        (shape(tokens, units), shape(tokens, D + LANES)),
        (lengths, grads, slope, second, first, *grams, *squares),
        2 * product,
        "last_back",
    )
    for kept, value in ((xs, x), (hiddens, hidden), (dzs, dz), (dys, grads)):
        kept.append(value)
    arrived = exchange(share.reshape(count, rows, D + LANES))
    own = grads.reshape(count, rows, D)
    grad_in, grad_out, results = final_products(
        lengths, arrived, own, results, xs, hiddens, dzs, dys
    )
    return grad_in[None], grad_out[None], results[None]


def solution(mesh):
    return jax.shard_map(
        per_device,
        mesh=mesh,
        in_specs=(
            P("section", None, "tensor", None),
            P("section", None),
            P("section", None, None),
            P("section", "tensor", None),
            P(None, "tensor", None),
            P("section", None, "tensor"),
            P("section", "tensor", None),
        ),
        out_specs=(
            P("section", None, "tensor"),
            P("section", "tensor", None),
            P("section", None, "tensor", None),
        ),
        check_vma=False,
    )
```

```python
import jax
import jax.numpy as jnp
from jax import lax
from jax.experimental import pallas as pl
from jax.experimental.pallas import tpu as pltpu
from jax.sharding import PartitionSpec as P

D = 1024
FF = 32768
GAMMA = 0.01
F32 = jnp.float32
BF16 = jnp.bfloat16
MIB = 1 << 20
STEP = 256
LANES = 128
SPACING = 32
ALONG_X = 4

VMEM = pl.BlockSpec(memory_space=pltpu.VMEM)


def shape(*dims, dtype=BF16):
    return jax.ShapeDtypeStruct(dims, dtype)


def call(kernel, outs, operands, flops, name, scratch=()):
    return pl.pallas_call(
        kernel,
        out_shape=outs,
        in_specs=[VMEM] * len(operands),
        out_specs=jax.tree.map(lambda _: VMEM, outs),
        scratch_shapes=[pltpu.VMEM(dims, BF16) for dims in scratch],
        name=name,
        compiler_params=pltpu.CompilerParams(vmem_limit_bytes=8 * MIB),
        cost_estimate=pl.CostEstimate(flops=flops, bytes_accessed=MIB, transcendentals=0),
    )(*operands)


def parts(extent):
    return [slice(at, at + STEP) for at in range(0, extent, STEP)]


def nt(a, b):
    return lax.dot_general(a, b, (((1,), (1,)), ((), ())), preferred_element_type=F32)


def tn(a, b):
    return lax.dot_general(a, b, (((0,), (0,)), ((), ())), preferred_element_type=F32)


def mm(a, b):
    return jnp.dot(a, b, preferred_element_type=F32)


def start_kernel(index, saved, grads, blocks_ref, index_v, saved_v, grads_v, sems):
    loads = [
        pltpu.make_async_copy(source, target, sems.at[place])
        for place, (source, target) in enumerate(
            ((index, index_v), (saved, saved_v), (grads, grads_v))
        )
    ]
    for load in loads:
        load.start()
    for load in loads:
        load.wait()
    count, rows, width = blocks_ref.shape
    for slot in range(index_v.shape[1]):
        wanted = index_v[:, slot : slot + 1]
        x = saved_v[0]
        for place in range(1, saved_v.shape[0]):
            x = jnp.where(wanted == place, saved_v[place], x)
        at = slot + 1 if slot else 0
        blocks_ref[:, :, D * at : D * (at + 1)] = jnp.broadcast_to(x[None], (count, rows, D))
    blocks_ref[:, :, D : 2 * D] = jnp.broadcast_to(grads_v[...][None], (count, rows, D))


def split_kernel(begun_ref, *out_refs):
    at = 0
    for out_ref in out_refs:
        width = out_ref.shape[-1]
        out_ref[...] = begun_ref[:, :, at : at + width]
        at += width


def assemble_kernel(*refs):
    blocks, out_refs = refs[:ALONG_X], refs[ALONG_X:]
    mine = lax.axis_index("tensor") % ALONG_X
    for distance, block_ref in enumerate(blocks):
        source = (mine + (ALONG_X - distance)) % ALONG_X
        for place, out_ref in enumerate(out_refs):
            out_ref[:, pl.ds(source, 1)] = block_ref[:, :, D * place : D * (place + 1)][:, None]


def forward_kernel(x_ref, weights_ref, slope_ref, hidden_ref):
    x = x_ref[...]
    for cols in parts(weights_ref.shape[1]):
        relu = jnp.maximum(mm(x, weights_ref[:, cols]), 0.0)
        slope_ref[:, cols] = 2.0 * relu
        hidden_ref[:, cols] = (relu * relu).astype(BF16)


def slope_kernel(x_ref, weights_ref, slope_ref):
    x = x_ref[...]
    for cols in parts(weights_ref.shape[1]):
        slope_ref[:, cols] = 2.0 * jnp.maximum(mm(x, weights_ref[:, cols]), 0.0)


def again_kernel(x_ref, grads_ref, w_in_ref, w_out_ref, hidden_ref, dz_ref):
    x, grads = x_ref[...], grads_ref[...]
    for part in parts(w_in_ref.shape[1]):
        relu = jnp.maximum(mm(x, w_in_ref[:, part]), 0.0)
        hidden_ref[:, part] = (relu * relu).astype(BF16)
        dz_ref[:, part] = (2.0 * relu * nt(grads, w_out_ref[part, :])).astype(BF16)


def masked_sums(slot, lengths_ref, paired):
    cut = lengths_ref[0:1, slot : slot + 1]
    tokens = paired.shape[0]
    row = lax.broadcasted_iota(jnp.int32, (tokens, tokens), 0) < cut
    col = lax.broadcasted_iota(jnp.int32, (tokens, tokens), 1) < cut
    before = jnp.sum(jnp.where(row & col, paired, 0.0), axis=(0, 1), keepdims=True)
    after = jnp.sum(jnp.where(row | col, 0.0, paired), axis=(0, 1), keepdims=True)
    lane = lax.broadcasted_iota(jnp.int32, (1, LANES), 1)
    return jnp.where(lane == 2 * slot, before, jnp.where(lane == 2 * slot + 1, after, 0.0))


def back_products(grads, slope_ref, w_out_ref, w_in_ref, dz_ref, share_ref):
    for part in parts(w_out_ref.shape[0]):
        back = nt(grads, w_out_ref[part, :])
        dz_ref[:, part] = (slope_ref[:, part] * back).astype(BF16)
    dz = dz_ref[...]
    for part in parts(w_in_ref.shape[0]):
        share_ref[:, part] = nt(dz, w_in_ref[part, :]).astype(BF16)
    return dz


def back_kernel(grads_ref, slope_ref, w_out_ref, w_in_ref, dz_ref, share_ref):
    back_products(grads_ref[...], slope_ref, w_out_ref, w_in_ref, dz_ref, share_ref)


def first_back_kernel(grads_ref, slope_ref, w_out_ref, w_in_ref, share_ref, dz_ref):
    back_products(grads_ref[...], slope_ref, w_out_ref, w_in_ref, dz_ref, share_ref)


def last_back_kernel(
    slot, lengths_ref, grads_ref, slope_ref, w_out_ref, w_in_ref, gram_x_ref, gram_h_ref, *refs
):
    *sums_refs, dz_ref, share_ref = refs
    grads = grads_ref[...]
    dz = back_products(grads, slope_ref, w_out_ref, w_in_ref, dz_ref, share_ref)
    paired = gram_x_ref[...] * nt(dz, dz) + gram_h_ref[...] * nt(grads, grads)
    total = masked_sums(slot, lengths_ref, paired)
    for sums_ref in sums_refs:
        total = total + sums_ref[...]
    high = total.astype(BF16)
    rest = total - high.astype(F32)
    middle = rest.astype(BF16)
    low = (rest - middle.astype(F32)).astype(BF16)
    line = high.astype(F32)
    for place, piece in ((1, middle), (2, low)):
        line = line + pltpu.roll(piece.astype(F32), place * SPACING, 1)
    share_ref[:, D:] = jnp.broadcast_to(line, (share_ref.shape[0], LANES)).astype(BF16)


def squares_kernel(slot, lengths_ref, x_ref, hidden_ref, grads_ref, dz_ref, sums_ref):
    x, hidden, grads, dz = x_ref[...], hidden_ref[...], grads_ref[...], dz_ref[...]
    paired = nt(x, x) * nt(dz, dz) + nt(hidden, hidden) * nt(grads, grads)
    sums_ref[...] = masked_sums(slot, lengths_ref, paired)


def grams_kernel(x_ref, hidden_ref, gram_x_ref, gram_h_ref):
    x, hidden = x_ref[...], hidden_ref[...]
    gram_x_ref[...] = nt(x, x)
    gram_h_ref[...] = nt(hidden, hidden)


def sum_kernel(place, arrived_ref, grads_ref, loss_ref, passing_ref, blocks_ref):
    own = lax.axis_index("tensor") if grads_ref.shape[0] > 1 else 0
    total = grads_ref[own].astype(F32)
    for peer in range(arrived_ref.shape[0]):
        total = total + arrived_ref[peer].astype(F32)
    passing = total.astype(BF16)
    passing_ref[...] = passing
    first = (lax.axis_index("section") == 0).astype(jnp.int32)
    chosen = jnp.where(jnp.full(passing.shape, first) > 0, loss_ref[place], passing)
    blocks_ref[...] = jnp.broadcast_to(chosen[None], blocks_ref.shape)


def final_kernel(slots, lengths_ref, arrived_ref, own_ref, *refs):
    earlier_refs, refs = refs[: slots - 1], refs[slots - 1 :]
    x, hidden, dz, dy = (refs[i * slots : (i + 1) * slots] for i in range(4))
    grad_in_ref, grad_out_ref, results_ref, dzc_ref, dyc_ref = refs[4 * slots :]
    tokens = dz[0].shape[0]
    step = pl.program_id(0)

    @pl.when(step == 0)
    def _():
        total = own_ref[lax.axis_index("tensor")].astype(F32)
        line = jnp.zeros((1, LANES), F32)
        for peer in range(arrived_ref.shape[0]):
            total = total + arrived_ref[peer, :, :D].astype(F32)
            line = line + arrived_ref[peer, 0:1, D:].astype(F32)
        for place, earlier_ref in enumerate(earlier_refs):
            results_ref[place] = earlier_ref[...]
        results_ref[slots - 1] = total.astype(BF16)
        pieces = [pltpu.roll(line, LANES - place * SPACING, 1) for place in (1, 2)]
        squares = line + (pieces[0] + pieces[1])
        factor = 1.0 / (jnp.sqrt(squares / (D * FF)) + GAMMA)
        for slot in range(slots):
            cut = lengths_ref[0:1, slot : slot + 1]
            row = lax.broadcasted_iota(jnp.int32, (tokens, 1), 0) < cut
            scale = jnp.where(
                row,
                factor[:, 2 * slot : 2 * slot + 1],
                factor[:, 2 * slot + 1 : 2 * slot + 2],
            )
            rows = slice(slot * tokens, (slot + 1) * tokens)
            dzc_ref[rows, :] = (dz[slot][...].astype(F32) * scale).astype(BF16)
            dyc_ref[rows, :] = (dy[slot][...].astype(F32) * scale).astype(BF16)

    block = grad_in_ref.shape[0]
    strip = pl.ds(pl.multiple_of(step * block, block), block)
    for left, right_ref, out_ref in ((x, dzc_ref, grad_in_ref), (hidden, dyc_ref, grad_out_ref)):
        lhs = jnp.concatenate([part[:, strip] for part in left], axis=0)
        for cols in parts(right_ref.shape[1]):
            out_ref[:, cols] = tn(lhs, right_ref[:, cols]).astype(BF16)


def final_products(lengths, arrived, own, earlier, x, hidden, dz, dy):
    slots = len(dz)
    tokens, width = dz[0].shape
    rows = x[0].shape[1]
    block = 512
    out = pl.BlockSpec((block, width), lambda i: (i, 0))
    results = shape(slots, *earlier[0].shape)
    return pl.pallas_call(
        lambda *refs: final_kernel(slots, *refs),
        grid=(rows // block,),
        out_shape=(shape(rows, width), shape(rows, width), results),
        in_specs=[VMEM] * (3 + slots - 1 + 4 * slots),
        out_specs=(out, out, pl.BlockSpec(results.shape, lambda i: (0, 0, 0))),
        scratch_shapes=[pltpu.VMEM((slots * tokens, width), BF16)] * 2,
        name="final",
        compiler_params=pltpu.CompilerParams(vmem_limit_bytes=16 * MIB),
        cost_estimate=pl.CostEstimate(
            flops=4 * rows * width * slots * tokens, bytes_accessed=4 * MIB, transcendentals=0
        ),
    )(lengths, arrived, own, *earlier, *x, *hidden, *dz, *dy)


def exchange(blocks):
    return lax.all_to_all(blocks, "tensor", split_axis=0, concat_axis=0, tiled=True)


def exchange_along_z(blocks):
    count = lax.axis_size("tensor")
    groups = [list(range(x, count, ALONG_X)) for x in range(ALONG_X)]
    return lax.all_to_all(
        blocks, "tensor", split_axis=0, concat_axis=0, axis_index_groups=groups, tiled=True
    )


def moved(value, sections_back, distance):
    sections, count = lax.axis_size("section"), lax.axis_size("tensor")
    pairs = [
        (
            section * count + at,
            (section - sections_back) % sections * count
            + at // ALONG_X * ALONG_X
            + (at + distance) % ALONG_X,
        )
        for section in range(sections)
        for at in range(count)
    ]
    return lax.ppermute(value, ("section", "tensor"), pairs)


def assemble(blocks):
    along_z, rows, width = blocks[0].shape
    outs = (shape(along_z, ALONG_X, rows, D),) * (width // D)
    gathered = call(assemble_kernel, outs, blocks, 0, "assemble")
    return [out.reshape(along_z * ALONG_X * rows, D) for out in gathered]


def per_device(saved_inputs, slot_index, example_lengths, first_grads, loss_grads, w_in, w_out):
    sections, count = lax.axis_size("section"), lax.axis_size("tensor")
    first, second = w_in[0], w_out[0]
    slots = loss_grads.shape[0] + 1
    rows = first_grads.shape[1]
    tokens = count * rows
    units = first.shape[1]
    lengths = example_lengths[0].T
    incoming = first_grads[0]
    product = 2 * tokens * D * units
    square = (tokens, tokens)

    along_z = count // ALONG_X
    blocks = pl.pallas_call(
        start_kernel,
        out_shape=shape(along_z, rows, (slots + 1) * D),
        in_specs=[pl.BlockSpec(memory_space=pl.ANY)] * 3,
        out_specs=VMEM,
        scratch_shapes=[
            pltpu.VMEM(slot_index.shape, jnp.int32),
            pltpu.VMEM(saved_inputs.shape[1:], BF16),
            pltpu.VMEM((rows, D), BF16),
            pltpu.SemaphoreType.DMA((3,)),
        ],
        name="start",
        compiler_params=pltpu.CompilerParams(vmem_limit_bytes=60 * MIB),
    )(slot_index, saved_inputs[0], incoming)
    begun = exchange_along_z(blocks)
    pieces = [shape(along_z, rows, width * D) for width in (1, 1, slots - 1)]
    x, grads, later = call(split_kernel, pieces, (begun,), 0, "split")
    x, grads, loss = lax.optimization_barrier((x, grads, loss_grads))
    x = [moved(x, 0, distance) if distance else x for distance in range(ALONG_X)]
    grads = [moved(grads, 0, distance) if distance else grads for distance in range(ALONG_X)]
    grads[0], loss = lax.optimization_barrier((grads[0], moved(loss, -1, 0)))
    [x], [grads] = assemble(x), assemble(grads)

    def forward(x):
        outs = (shape(tokens, units, dtype=F32), shape(tokens, units))
        return call(forward_kernel, outs, (x, first), product, "forward")

    slope = call(
        slope_kernel, shape(tokens, units, dtype=F32), (x, first), product, "slope"
    )
    xs, hiddens, dzs, dys, results, squares = [], [], [], [], [], []
    for slot in range(slots - 1):
        if slot:
            dz, share = call(
                back_kernel,
                (shape(tokens, units), shape(tokens, D)),
                (grads, slope, second, first),
                2 * product,
                "back",
            )
            own = grads.reshape(count, rows, D)
        else:
            share = call(
                first_back_kernel,
                shape(tokens, D),
                (grads, slope, second, first),
                2 * product,
                "first_back",
                scratch=[(tokens, units)],
            )
            own = first_grads
        arrived = exchange(share.reshape(count, rows, D))
        if slot == 0:
            blocks = [later] + [moved(later, 0, distance) for distance in range(1, ALONG_X)]
            later = assemble(blocks)
        passing, blocks = call(
            lambda *refs, slot=slot: sum_kernel(slot, *refs),
            (shape(rows, D), shape(along_z, rows, D)),
            (arrived, own, loss),
            tokens * D,
            "add_up",
        )
        results.append(passing)
        block = exchange_along_z(blocks)
        pieces = [moved(block, 1, distance) for distance in range(ALONG_X)]
        made = (hidden, dz) if slot else (first, second)
        _, next_x, x, grads, *made = lax.optimization_barrier(
            (block, later[slot], x, grads, *made)
        )
        if slot:
            hidden, dz = made
        else:
            hidden, dz = call(
                again_kernel, (shape(tokens, units),) * 2, (x, grads, *made), 0, "again"
            )
        for kept, value in ((xs, x), (hiddens, hidden), (dzs, dz), (dys, grads)):
            kept.append(value)
        one = call(
            lambda *refs, slot=slot: squares_kernel(slot, *refs),
            shape(1, LANES, dtype=F32),
            (lengths, x, hidden, grads, dz),
            product,
            "squares",
        )
        x = next_x
        squares.append(one)
        slope, hidden = forward(x)
        ready = [one, slope, hidden]
        if slot + 2 == slots:
            ready += call(
                grams_kernel, (shape(*square, dtype=F32),) * 2, (x, hidden), product // 4, "grams"
            )
        pieces[0], squares[-1], slope, hidden, *grams = lax.optimization_barrier(
            (pieces[0], *ready)
        )
        [grads] = assemble(pieces)

    dz, share = call(
        lambda *refs: last_back_kernel(slots - 1, *refs),
        (shape(tokens, units), shape(tokens, D + LANES)),
        (lengths, grads, slope, second, first, *grams, *squares),
        2 * product,
        "last_back",
    )
    for kept, value in ((xs, x), (hiddens, hidden), (dzs, dz), (dys, grads)):
        kept.append(value)
    arrived = exchange(share.reshape(count, rows, D + LANES))
    own = grads.reshape(count, rows, D)
    grad_in, grad_out, results = final_products(
        lengths, arrived, own, results, xs, hiddens, dzs, dys
    )
    return grad_in[None], grad_out[None], results[None]


def solution(mesh):
    return jax.shard_map(
        per_device,
        mesh=mesh,
        in_specs=(
            P("section", None, "tensor", None),
            P("section", None),
            P("section", None, None),
            P("section", "tensor", None),
            P(None, "tensor", None),
            P("section", None, "tensor"),
            P("section", "tensor", None),
        ),
        out_specs=(
            P("section", None, "tensor"),
            P("section", "tensor", None),
            P("section", None, "tensor", None),
        ),
        check_vma=False,
    )
```

```python
import jax
import jax.numpy as jnp
from jax import lax
from jax.experimental import pallas as pl
from jax.experimental.pallas import tpu as pltpu
from jax.sharding import PartitionSpec as P

D = 1024
FF = 32768
GAMMA = 0.01
F32 = jnp.float32
BF16 = jnp.bfloat16
MIB = 1 << 20
STEP = 256
LANES = 128
SPACING = 32
ALONG_X = 4

VMEM = pl.BlockSpec(memory_space=pltpu.VMEM)


def shape(*dims, dtype=BF16):
    return jax.ShapeDtypeStruct(dims, dtype)


def call(kernel, outs, operands, flops, name, scratch=()):
    return pl.pallas_call(
        kernel,
        out_shape=outs,
        in_specs=[VMEM] * len(operands),
        out_specs=jax.tree.map(lambda _: VMEM, outs),
        scratch_shapes=[pltpu.VMEM(dims, BF16) for dims in scratch],
        name=name,
        compiler_params=pltpu.CompilerParams(vmem_limit_bytes=8 * MIB),
        cost_estimate=pl.CostEstimate(flops=flops, bytes_accessed=MIB, transcendentals=0),
    )(*operands)


def parts(extent):
    return [slice(at, at + STEP) for at in range(0, extent, STEP)]


def nt(a, b):
    return lax.dot_general(a, b, (((1,), (1,)), ((), ())), preferred_element_type=F32)


def tn(a, b):
    return lax.dot_general(a, b, (((0,), (0,)), ((), ())), preferred_element_type=F32)


def mm(a, b):
    return jnp.dot(a, b, preferred_element_type=F32)


def start_kernel(index, saved, grads, blocks_ref, index_v, saved_v, grads_v, sems):
    loads = [
        pltpu.make_async_copy(source, target, sems.at[place])
        for place, (source, target) in enumerate(
            ((index, index_v), (saved, saved_v), (grads, grads_v))
        )
    ]
    for load in loads:
        load.start()
    for load in loads:
        load.wait()
    count, rows, width = blocks_ref.shape
    for slot in range(index_v.shape[1]):
        wanted = index_v[:, slot : slot + 1]
        x = saved_v[0]
        for place in range(1, saved_v.shape[0]):
            x = jnp.where(wanted == place, saved_v[place], x)
        at = slot + 1 if slot else 0
        blocks_ref[:, :, D * at : D * (at + 1)] = jnp.broadcast_to(x[None], (count, rows, D))
    blocks_ref[:, :, D : 2 * D] = jnp.broadcast_to(grads_v[...][None], (count, rows, D))


def split_kernel(begun_ref, *out_refs):
    at = 0
    for out_ref in out_refs:
        width = out_ref.shape[-1]
        out_ref[...] = begun_ref[:, :, at : at + width]
        at += width


def assemble_kernel(*refs):
    blocks, out_refs = refs[:ALONG_X], refs[ALONG_X:]
    mine = lax.axis_index("tensor") % ALONG_X
    for distance, block_ref in enumerate(blocks):
        source = (mine + (ALONG_X - distance)) % ALONG_X
        for place, out_ref in enumerate(out_refs):
            out_ref[:, pl.ds(source, 1)] = block_ref[:, :, D * place : D * (place + 1)][:, None]


def forward_kernel(x_ref, weights_ref, slope_ref, hidden_ref):
    x = x_ref[...]
    for cols in parts(weights_ref.shape[1]):
        relu = jnp.maximum(mm(x, weights_ref[:, cols]), 0.0)
        slope_ref[:, cols] = 2.0 * relu
        hidden_ref[:, cols] = (relu * relu).astype(BF16)


def slope_kernel(x_ref, weights_ref, slope_ref):
    x = x_ref[...]
    for cols in parts(weights_ref.shape[1]):
        slope_ref[:, cols] = 2.0 * jnp.maximum(mm(x, weights_ref[:, cols]), 0.0)


def again_kernel(x_ref, grads_ref, w_in_ref, w_out_ref, hidden_ref, dz_ref):
    x, grads = x_ref[...], grads_ref[...]
    for part in parts(w_in_ref.shape[1]):
        relu = jnp.maximum(mm(x, w_in_ref[:, part]), 0.0)
        hidden_ref[:, part] = (relu * relu).astype(BF16)
        dz_ref[:, part] = (2.0 * relu * nt(grads, w_out_ref[part, :])).astype(BF16)


def masked_sums(slot, lengths_ref, paired):
    cut = lengths_ref[0:1, slot : slot + 1]
    tokens = paired.shape[0]
    row = lax.broadcasted_iota(jnp.int32, (tokens, tokens), 0) < cut
    col = lax.broadcasted_iota(jnp.int32, (tokens, tokens), 1) < cut
    before = jnp.sum(jnp.where(row & col, paired, 0.0), axis=(0, 1), keepdims=True)
    after = jnp.sum(jnp.where(row | col, 0.0, paired), axis=(0, 1), keepdims=True)
    lane = lax.broadcasted_iota(jnp.int32, (1, LANES), 1)
    return jnp.where(lane == 2 * slot, before, jnp.where(lane == 2 * slot + 1, after, 0.0))


def back_products(grads, slope_ref, w_out_ref, w_in_ref, dz_ref, share_ref):
    for part in parts(w_out_ref.shape[0]):
        back = nt(grads, w_out_ref[part, :])
        dz_ref[:, part] = (slope_ref[:, part] * back).astype(BF16)
    dz = dz_ref[...]
    for part in parts(w_in_ref.shape[0]):
        share_ref[:, part] = nt(dz, w_in_ref[part, :]).astype(BF16)
    return dz


def back_kernel(grads_ref, slope_ref, w_out_ref, w_in_ref, dz_ref, share_ref):
    back_products(grads_ref[...], slope_ref, w_out_ref, w_in_ref, dz_ref, share_ref)


def first_back_kernel(grads_ref, slope_ref, w_out_ref, w_in_ref, share_ref, dz_ref):
    back_products(grads_ref[...], slope_ref, w_out_ref, w_in_ref, dz_ref, share_ref)


def last_back_kernel(
    slot, lengths_ref, grads_ref, slope_ref, w_out_ref, w_in_ref, gram_x_ref, gram_h_ref, *refs
):
    *sums_refs, dz_ref, share_ref = refs
    grads = grads_ref[...]
    dz = back_products(grads, slope_ref, w_out_ref, w_in_ref, dz_ref, share_ref)
    paired = gram_x_ref[...] * nt(dz, dz) + gram_h_ref[...] * nt(grads, grads)
    total = masked_sums(slot, lengths_ref, paired)
    for sums_ref in sums_refs:
        total = total + sums_ref[...]
    high = total.astype(BF16)
    rest = total - high.astype(F32)
    middle = rest.astype(BF16)
    low = (rest - middle.astype(F32)).astype(BF16)
    line = high.astype(F32)
    for place, piece in ((1, middle), (2, low)):
        line = line + pltpu.roll(piece.astype(F32), place * SPACING, 1)
    share_ref[:, D:] = jnp.broadcast_to(line, (share_ref.shape[0], LANES)).astype(BF16)


def squares_kernel(slot, lengths_ref, x_ref, hidden_ref, grads_ref, dz_ref, sums_ref):
    x, hidden, grads, dz = x_ref[...], hidden_ref[...], grads_ref[...], dz_ref[...]
    paired = nt(x, x) * nt(dz, dz) + nt(hidden, hidden) * nt(grads, grads)
    sums_ref[...] = masked_sums(slot, lengths_ref, paired)


def grams_kernel(x_ref, hidden_ref, gram_x_ref, gram_h_ref):
    x, hidden = x_ref[...], hidden_ref[...]
    gram_x_ref[...] = nt(x, x)
    gram_h_ref[...] = nt(hidden, hidden)


def sum_kernel(place, arrived_ref, grads_ref, loss_ref, passing_ref, blocks_ref):
    own = lax.axis_index("tensor") if grads_ref.shape[0] > 1 else 0
    total = grads_ref[own].astype(F32)
    for peer in range(arrived_ref.shape[0]):
        total = total + arrived_ref[peer].astype(F32)
    passing = total.astype(BF16)
    passing_ref[...] = passing
    first = (lax.axis_index("section") == 0).astype(jnp.int32)
    chosen = jnp.where(jnp.full(passing.shape, first) > 0, loss_ref[place], passing)
    blocks_ref[...] = jnp.broadcast_to(chosen[None], blocks_ref.shape)


def final_kernel(slots, lengths_ref, arrived_ref, own_ref, *refs):
    earlier_refs, refs = refs[: slots - 1], refs[slots - 1 :]
    x, hidden, dz, dy = (refs[i * slots : (i + 1) * slots] for i in range(4))
    grad_in_ref, grad_out_ref, results_ref, dzc_ref, dyc_ref = refs[4 * slots :]
    tokens = dz[0].shape[0]
    step = pl.program_id(0)

    @pl.when(step == 0)
    def _():
        total = own_ref[lax.axis_index("tensor")].astype(F32)
        line = jnp.zeros((1, LANES), F32)
        for peer in range(arrived_ref.shape[0]):
            total = total + arrived_ref[peer, :, :D].astype(F32)
            line = line + arrived_ref[peer, 0:1, D:].astype(F32)
        for place, earlier_ref in enumerate(earlier_refs):
            results_ref[place] = earlier_ref[...]
        results_ref[slots - 1] = total.astype(BF16)
        pieces = [pltpu.roll(line, LANES - place * SPACING, 1) for place in (1, 2)]
        squares = line + (pieces[0] + pieces[1])
        factor = 1.0 / (jnp.sqrt(squares / (D * FF)) + GAMMA)
        for slot in range(slots):
            cut = lengths_ref[0:1, slot : slot + 1]
            row = lax.broadcasted_iota(jnp.int32, (tokens, 1), 0) < cut
            scale = jnp.where(
                row,
                factor[:, 2 * slot : 2 * slot + 1],
                factor[:, 2 * slot + 1 : 2 * slot + 2],
            )
            rows = slice(slot * tokens, (slot + 1) * tokens)
            dzc_ref[rows, :] = (dz[slot][...].astype(F32) * scale).astype(BF16)
            dyc_ref[rows, :] = (dy[slot][...].astype(F32) * scale).astype(BF16)

    block = grad_in_ref.shape[0]
    strip = pl.ds(pl.multiple_of(step * block, block), block)
    for left, right_ref, out_ref in ((x, dzc_ref, grad_in_ref), (hidden, dyc_ref, grad_out_ref)):
        lhs = jnp.concatenate([part[:, strip] for part in left], axis=0)
        for cols in parts(right_ref.shape[1]):
            out_ref[:, cols] = tn(lhs, right_ref[:, cols]).astype(BF16)


def final_products(lengths, arrived, own, earlier, x, hidden, dz, dy):
    slots = len(dz)
    tokens, width = dz[0].shape
    rows = x[0].shape[1]
    block = 512
    out = pl.BlockSpec((block, width), lambda i: (i, 0))
    results = shape(slots, *earlier[0].shape)
    return pl.pallas_call(
        lambda *refs: final_kernel(slots, *refs),
        grid=(rows // block,),
        out_shape=(shape(rows, width), shape(rows, width), results),
        in_specs=[VMEM] * (3 + slots - 1 + 4 * slots),
        out_specs=(out, out, pl.BlockSpec(results.shape, lambda i: (0, 0, 0))),
        scratch_shapes=[pltpu.VMEM((slots * tokens, width), BF16)] * 2,
        name="final",
        compiler_params=pltpu.CompilerParams(vmem_limit_bytes=16 * MIB),
        cost_estimate=pl.CostEstimate(
            flops=4 * rows * width * slots * tokens, bytes_accessed=4 * MIB, transcendentals=0
        ),
    )(lengths, arrived, own, *earlier, *x, *hidden, *dz, *dy)


def exchange(blocks):
    return lax.all_to_all(blocks, "tensor", split_axis=0, concat_axis=0, tiled=True)


def exchange_along_z(blocks):
    count = lax.axis_size("tensor")
    groups = [list(range(x, count, ALONG_X)) for x in range(ALONG_X)]
    return lax.all_to_all(
        blocks, "tensor", split_axis=0, concat_axis=0, axis_index_groups=groups, tiled=True
    )


def moved(value, sections_back, distance):
    sections, count = lax.axis_size("section"), lax.axis_size("tensor")
    pairs = [
        (
            section * count + at,
            (section - sections_back) % sections * count
            + at // ALONG_X * ALONG_X
            + (at + distance) % ALONG_X,
        )
        for section in range(sections)
        for at in range(count)
    ]
    return lax.ppermute(value, ("section", "tensor"), pairs)


def assemble(blocks):
    along_z, rows, width = blocks[0].shape
    outs = (shape(along_z, ALONG_X, rows, D),) * (width // D)
    gathered = call(assemble_kernel, outs, blocks, 0, "assemble")
    return [out.reshape(along_z * ALONG_X * rows, D) for out in gathered]


def per_device(saved_inputs, slot_index, example_lengths, first_grads, loss_grads, w_in, w_out):
    sections, count = lax.axis_size("section"), lax.axis_size("tensor")
    first, second = w_in[0], w_out[0]
    slots = loss_grads.shape[0] + 1
    rows = first_grads.shape[1]
    tokens = count * rows
    units = first.shape[1]
    lengths = example_lengths[0].T
    incoming = first_grads[0]
    product = 2 * tokens * D * units
    square = (tokens, tokens)

    along_z = count // ALONG_X
    blocks = pl.pallas_call(
        start_kernel,
        out_shape=shape(along_z, rows, (slots + 1) * D),
        in_specs=[pl.BlockSpec(memory_space=pl.ANY)] * 3,
        out_specs=VMEM,
        scratch_shapes=[
            pltpu.VMEM(slot_index.shape, jnp.int32),
            pltpu.VMEM(saved_inputs.shape[1:], BF16),
            pltpu.VMEM((rows, D), BF16),
            pltpu.SemaphoreType.DMA((3,)),
        ],
        name="start",
        compiler_params=pltpu.CompilerParams(vmem_limit_bytes=60 * MIB),
    )(slot_index, saved_inputs[0], incoming)
    begun = exchange_along_z(blocks)
    pieces = [shape(along_z, rows, width * D) for width in (1, 1, slots - 1)]
    x, grads, later = call(split_kernel, pieces, (begun,), 0, "split")
    x = [moved(x, 0, distance) if distance else x for distance in range(ALONG_X)]
    grads = [moved(grads, 0, distance) if distance else grads for distance in range(ALONG_X)]
    loss = moved(loss_grads, -1, 0)
    [x], [grads] = assemble(x), assemble(grads)

    def forward(x):
        outs = (shape(tokens, units, dtype=F32), shape(tokens, units))
        return call(forward_kernel, outs, (x, first), product, "forward")

    slope = call(
        slope_kernel, shape(tokens, units, dtype=F32), (x, first), product, "slope"
    )
    xs, hiddens, dzs, dys, results, squares = [], [], [], [], [], []
    for slot in range(slots - 1):
        if slot:
            dz, share = call(
                back_kernel,
                (shape(tokens, units), shape(tokens, D)),
                (grads, slope, second, first),
                2 * product,
                "back",
            )
            own = grads.reshape(count, rows, D)
        else:
            share = call(
                first_back_kernel,
                shape(tokens, D),
                (grads, slope, second, first),
                2 * product,
                "first_back",
                scratch=[(tokens, units)],
            )
            own = first_grads
        arrived = exchange(share.reshape(count, rows, D))
        if slot == 0:
            blocks = [later] + [moved(later, 0, distance) for distance in range(1, ALONG_X)]
            later = assemble(blocks)
        passing, blocks = call(
            lambda *refs, slot=slot: sum_kernel(slot, *refs),
            (shape(rows, D), shape(along_z, rows, D)),
            (arrived, own, loss),
            tokens * D,
            "add_up",
        )
        results.append(passing)
        block = exchange_along_z(blocks)
        pieces = [moved(block, 1, distance) for distance in range(ALONG_X)]
        made = (hidden, dz) if slot else (first, second)
        _, next_x, x, grads, *made = lax.optimization_barrier(
            (block, later[slot], x, grads, *made)
        )
        if slot:
            hidden, dz = made
        else:
            hidden, dz = call(
                again_kernel, (shape(tokens, units),) * 2, (x, grads, *made), 0, "again"
            )
        for kept, value in ((xs, x), (hiddens, hidden), (dzs, dz), (dys, grads)):
            kept.append(value)
        one = call(
            lambda *refs, slot=slot: squares_kernel(slot, *refs),
            shape(1, LANES, dtype=F32),
            (lengths, x, hidden, grads, dz),
            product,
            "squares",
        )
        x = next_x
        squares.append(one)
        slope, hidden = forward(x)
        ready = [one, slope, hidden]
        if slot + 2 == slots:
            ready += call(
                grams_kernel, (shape(*square, dtype=F32),) * 2, (x, hidden), product // 4, "grams"
            )
        pieces[0], squares[-1], slope, hidden, *grams = lax.optimization_barrier(
            (pieces[0], *ready)
        )
        [grads] = assemble(pieces)

    dz, share = call(
        lambda *refs: last_back_kernel(slots - 1, *refs),
        (shape(tokens, units), shape(tokens, D + LANES)),
        (lengths, grads, slope, second, first, *grams, *squares),
        2 * product,
        "last_back",
    )
    for kept, value in ((xs, x), (hiddens, hidden), (dzs, dz), (dys, grads)):
        kept.append(value)
    arrived = exchange(share.reshape(count, rows, D + LANES))
    own = grads.reshape(count, rows, D)
    grad_in, grad_out, results = final_products(
        lengths, arrived, own, results, xs, hiddens, dzs, dys
    )
    return grad_in[None], grad_out[None], results[None]


def solution(mesh):
    return jax.shard_map(
        per_device,
        mesh=mesh,
        in_specs=(
            P("section", None, "tensor", None),
            P("section", None),
            P("section", None, None),
            P("section", "tensor", None),
            P(None, "tensor", None),
            P("section", None, "tensor"),
            P("section", "tensor", None),
        ),
        out_specs=(
            P("section", None, "tensor"),
            P("section", "tensor", None),
            P("section", None, "tensor", None),
        ),
        check_vma=False,
    )
```
